128 devices in a mesh: ka: 8 (over y, z_lo), rp: 16 (over z_hi, x, core).
Axes of the slice: x: 4, y: 4, z: 4 (z_hi: 2, z_lo: 2; z = z_hi * 2 + z_lo), core: 2. Of those that a mesh axis runs over, the one named last changes fastest.
Arguments:
- coupling_table: bfloat16 [512, 256, 1024], P('ka', 'rp'), may hold values from -0.016479492 to 0.016479492
- k_points: int32 [3, 4096], P(None, 'ka'), may hold values from 0 to 15
- re_vectors: int32 [3, 512], replicated, may hold values from -6 to 6
- rp_vectors: int32 [3, 256], P(None, 'rp'), may hold values from -6 to 6
- q_points: int32 [3, 2], replicated, may hold values from 0 to 15
Outputs:
- bloch_coupling: float32 [4096, 2048], P(('ka', 'rp'))
The draws below stay inside these ranges and needn't reach their ends.
All inputs are finite; a program needn't handle non-finite values.
Results may differ from the reference program's by a relative error of at most 0.0022.
Values may be sent and summed in bfloat16 or wider, within the bound.
No kernel may reach another device: no remote copies, remote signals or barrier semaphores. Data moves between devices by JAX's collectives and lax.ppermute only.
A program may use at most 64 MiB of HBM per device.

```python
import math
import jax
import jax.numpy as jnp
from jax import lax

RE = 512
RP = 256
M = 512
Q = 2
NKG = 16
KTOT = 4096


def place_ends(values, rng, smallest, high):
    index_at = [jax.random.randint(jax.random.fold_in(rng, axis), (), 0, length) for axis, length in enumerate(values.shape)]
    main_axis = values.shape.index(max(values.shape))
    neighbour = index_at[:main_axis] + [(index_at[main_axis] + 1) % values.shape[main_axis]] + index_at[main_axis + 1:]
    return values.at[tuple(index_at)].set(smallest).at[tuple(neighbour)].set(high)


def shard_levels(own_key, dims, cuts, smallest, largest):
    level = 1.0
    for position, parts in cuts:
        draws = jax.random.uniform(jax.random.fold_in(jax.random.fold_in(own_key, 6), position), (parts,), jnp.float32, smallest / len(cuts), largest / len(cuts))
        level = level * jnp.repeat(jnp.exp(draws), dims[position] // parts).reshape((-1,) + (1,) * (len(dims) - 1 - position))
    return level


def noise(rng, shape, scale, most, cuts=(), held_as=jnp.bfloat16):
    result = jax.random.normal(rng, shape, jnp.float32) * scale
    if len(cuts) > 0:
        result = shard_levels(rng, shape, cuts, -0.22, 0.18) * result
    return jnp.clip(result, min=-most, max=most).astype(held_as)


def setup_inputs(seed: int = 0) -> dict:
    streams_of = jax.random.split(jax.random.key(seed), 6)
    coupling_table = noise(streams_of[0], (RE, RP, 2 * M), 0.00275, 0.016479492, ((0, 8), (1, 16)))
    k_points = place_ends(jax.random.randint(streams_of[1], (3, KTOT), 0, NKG), jax.random.fold_in(streams_of[1], 1), 0, NKG - 1).astype(jnp.int32)
    re_vectors = place_ends(jax.random.randint(streams_of[2], (3, RE), -6, 7), jax.random.fold_in(streams_of[2], 1), -6, 6).astype(jnp.int32)
    rp_vectors = place_ends(jax.random.randint(streams_of[3], (3, RP), -6, 7), jax.random.fold_in(streams_of[3], 1), -6, 6).astype(jnp.int32)
    q_points = place_ends(jax.random.randint(streams_of[4], (3, Q), 0, NKG), jax.random.fold_in(streams_of[4], 1), 0, NKG - 1).astype(jnp.int32)
    return dict(coupling_table=coupling_table, k_points=k_points, re_vectors=re_vectors, rp_vectors=rp_vectors, q_points=q_points)


def phases(left, right):
    nested = left[0][:, None] * right[0][None, :] + left[1][:, None] * right[1][None, :] + left[2][:, None] * right[2][None, :]
    wrapped = jnp.mod(nested, NKG).astype(jnp.int32)
    angles = wrapped.astype(jnp.float32) * (2.0 * math.pi / NKG)
    return jnp.cos(angles), jnp.sin(angles)


def reference(coupling_table, k_points, re_vectors, rp_vectors, q_points):
    high = lax.Precision.HIGHEST
    q_cos, q_sin = phases(q_points, rp_vectors)
    values = coupling_table.astype(jnp.float32).reshape(RE, RP, 2, M)
    real_in = values[:, :, 0, :]
    imag_in = values[:, :, 1, :]
    real_mid = jnp.einsum("qr,erm->eqm", q_cos, real_in, precision=high) - jnp.einsum("qr,erm->eqm", q_sin, imag_in, precision=high)
    imag_mid = jnp.einsum("qr,erm->eqm", q_sin, real_in, precision=high) + jnp.einsum("qr,erm->eqm", q_cos, imag_in, precision=high)
    real_mid = real_mid.reshape(RE, Q * M)
    imag_mid = imag_mid.reshape(RE, Q * M)
    k_cos, k_sin = phases(k_points, re_vectors)
    k_cos = k_cos.astype(jnp.bfloat16).astype(jnp.float32)
    k_sin = k_sin.astype(jnp.bfloat16).astype(jnp.float32)
    real_out = jnp.dot(k_cos, real_mid, precision=high, preferred_element_type=jnp.float32) - jnp.dot(k_sin, imag_mid, precision=high, preferred_element_type=jnp.float32)
    imag_out = jnp.dot(k_sin, real_mid, precision=high, preferred_element_type=jnp.float32) + jnp.dot(k_cos, imag_mid, precision=high, preferred_element_type=jnp.float32)
    return jnp.stack([real_out, imag_out], axis=1).reshape(KTOT, 2 * Q * M)
```

```python
import functools
import math

import jax
import jax.numpy as jnp
from jax import lax
from jax.experimental import pallas as pl
from jax.experimental.pallas import tpu as pltpu
from jax.sharding import PartitionSpec as P

NKG = 16
LANES = 128
HALF = 64
QUARTER = [math.cos(2.0 * math.pi * n / NKG) for n in range(4)] + [0.0]


def cosine(n):
    m = n & (NKG - 1)
    t = jnp.minimum(m, NKG - m)
    u = jnp.minimum(t, 8 - t)
    value = jnp.full(n.shape, QUARTER[0], jnp.float32)
    for i in range(1, 5):
        value = jnp.where(u == i, jnp.float32(QUARTER[i]), value)
    return jnp.where(t > 4, -value, value)


def wave_sums(q_ref, rp_ref, table_ref, out_ref, weights_ref):
    groups = weights_ref.shape[1] // 16

    @pl.when(pl.program_id(0) == 0)
    def _():
        lane = lax.broadcasted_iota(jnp.int32, (16, 256), 1)
        row = lax.broadcasted_iota(jnp.int32, (16, 256), 0)
        spread = jnp.where((lane & 15) == row, 1.0, 0.0).astype(jnp.bfloat16)
        vectors = jnp.dot(
            rp_ref[...].astype(jnp.float32).astype(jnp.bfloat16),
            spread,
            preferred_element_type=jnp.float32,
        ).astype(jnp.int32)
        own = (lane >> 4) == row
        for q in range(2):
            n = (
                q_ref[0, q] * vectors[0:1]
                + q_ref[1, q] * vectors[1:2]
                + q_ref[2, q] * vectors[2:3]
            )
            for part, value in enumerate((cosine(n), cosine(n - 4))):
                high = value.astype(jnp.bfloat16).astype(jnp.float32)
                for fine, piece in enumerate((high, value - high)):
                    at = 64 * fine + 32 * part + 16 * q
                    block = jnp.where(own, jnp.broadcast_to(piece, (16, 256)), 0.0)
                    weights_ref[at : at + 16, :] = block.astype(jnp.bfloat16)

    y = jnp.dot(weights_ref[...], table_ref[...], preferred_element_type=jnp.float32)
    y = y[:64] + y[64:]
    by_cos, by_sin = y[:32], y[32:]
    real = by_cos[:, :512] - by_sin[:, 512:]
    imag = by_sin[:, :512] + by_cos[:, 512:]
    low = lax.broadcasted_iota(jnp.int32, (16, LANES), 1) < HALF
    for q in range(2):
        for b in range(4):
            re = real[16 * q : 16 * q + 16, LANES * b : LANES * (b + 1)]
            im = imag[16 * q : 16 * q + 16, LANES * b : LANES * (b + 1)]
            first = jnp.where(low, re, pltpu.roll(im, HALF, 1))
            second = jnp.where(low, pltpu.roll(re, HALF, 1), im)
            out_ref[8 * q + 2 * b] = first.astype(out_ref.dtype)
            out_ref[8 * q + 2 * b + 1] = second.astype(out_ref.dtype)


def add_parts(parts_ref, out_ref):
    total = parts_ref[0].astype(jnp.float32)
    for r in range(1, parts_ref.shape[0]):
        total = total + parts_ref[r].astype(jnp.float32)
    high = total.astype(jnp.bfloat16)
    low = (total - high.astype(jnp.float32)).astype(jnp.bfloat16)
    for a in range(out_ref.shape[0]):
        out_ref[a, 0] = high
        out_ref[a, 1] = low


def bloch(mid_ref, k_ref, re_ref, out_ref, phase_ref):
    k = k_ref[...].astype(jnp.float32).astype(jnp.bfloat16)
    re = re_ref[...].astype(jnp.float32).astype(jnp.bfloat16)
    n = lax.dot_general(k, re, (((0,), (0,)), ((), ())), preferred_element_type=jnp.float32)
    n = n.astype(jnp.int32)
    phase_ref[:, :512] = cosine(n).astype(jnp.bfloat16)
    phase_ref[:, 512:] = cosine(n - 4).astype(jnp.bfloat16)
    low = lax.broadcasted_iota(jnp.int32, (512, LANES), 1) < HALF
    straight, turned = [], []
    for piece in range(2):
        x = mid_ref[:, piece].reshape(512, LANES).astype(jnp.float32)
        rolled = pltpu.roll(x, HALF, 1)
        straight.append(x)
        turned.append(jnp.where(low, -rolled, rolled))
    with_cos = jnp.concatenate(straight, axis=1).astype(jnp.bfloat16)
    with_sin = jnp.concatenate(turned, axis=1).astype(jnp.bfloat16)
    out = jnp.dot(phase_ref[:, :512], with_cos, preferred_element_type=jnp.float32)
    out = out + jnp.dot(phase_ref[:, 512:], with_sin, preferred_element_type=jnp.float32)
    out_ref[...] = out[:, :LANES] + out[:, LANES:]


def place(pieces_ref, out_ref):
    low = lax.broadcasted_iota(jnp.int32, (32, LANES), 1) < HALF
    for pair in range(8):
        x0 = pieces_ref[2 * pair].astype(jnp.float32)
        x1 = pieces_ref[2 * pair + 1].astype(jnp.float32)
        at = LANES * pair
        out_ref[:, at : at + LANES] = jnp.where(low, x0, pltpu.roll(x1, HALF, 1))
        out_ref[:, 1024 + at : 1024 + at + LANES] = jnp.where(low, pltpu.roll(x0, HALF, 1), x1)


def per_device(coupling_table, k_points, re_vectors, rp_vectors, q_points):
    vmem = pl.BlockSpec(memory_space=pltpu.VMEM)
    smem = pl.BlockSpec(memory_space=pltpu.SMEM)
    table = coupling_table.reshape(1024, 1024)
    parts = pl.pallas_call(
        wave_sums,
        grid=(4,),
        in_specs=[smem, vmem, pl.BlockSpec((256, 1024), lambda g: (g, 0))],
        out_specs=pl.BlockSpec((16, 16, LANES), lambda g: (0, g, 0)),
        out_shape=jax.ShapeDtypeStruct((16, 64, LANES), jnp.bfloat16),
        scratch_shapes=[pltpu.VMEM((128, 256), jnp.bfloat16)],
        name="wave_sums",
    )(q_points, rp_vectors, table)
    parts = lax.all_to_all(parts, "rp", 0, 0, tiled=True)
    mid = pl.pallas_call(
        add_parts,
        in_specs=[vmem],
        out_specs=vmem,
        out_shape=jax.ShapeDtypeStruct((8, 2, 64, LANES), jnp.bfloat16),
        name="add_parts",
    )(parts)
    mid = lax.all_to_all(mid, "ka", 0, 0, tiled=True)
    columns = pl.pallas_call(
        bloch,
        in_specs=[vmem, vmem, vmem],
        out_specs=vmem,
        out_shape=jax.ShapeDtypeStruct((512, LANES), jnp.float32),
        scratch_shapes=[pltpu.VMEM((512, 1024), jnp.bfloat16)],
        name="bloch",
    )(mid, k_points, re_vectors)
    pieces = lax.all_to_all(columns.reshape(16, 32, LANES), "rp", 0, 0, tiled=True)
    return pl.pallas_call(
        place,
        in_specs=[vmem],
        out_specs=vmem,
        out_shape=jax.ShapeDtypeStruct((32, 2048), jnp.float32),
        name="place",
    )(pieces)


def solution(mesh):
    placed = (P("ka", "rp", None), P(None, "ka"), P(), P(None, "rp"), P())
    return jax.shard_map(
        per_device, mesh=mesh, in_specs=placed, out_specs=P(("ka", "rp"), None), check_vma=False
    )
```

```python
import functools
import math

import jax
import jax.numpy as jnp
from jax import lax
from jax.experimental import pallas as pl
from jax.experimental.pallas import tpu as pltpu
from jax.sharding import PartitionSpec as P

NKG = 16
LANES = 128
HALF = 64
QUARTER = [math.cos(2.0 * math.pi * n / NKG) for n in range(4)] + [0.0]


def cosine(n):
    m = n & (NKG - 1)
    t = jnp.minimum(m, NKG - m)
    u = jnp.minimum(t, 8 - t)
    value = jnp.full(n.shape, QUARTER[0], jnp.float32)
    for i in range(1, 5):
        value = jnp.where(u == i, jnp.float32(QUARTER[i]), value)
    return jnp.where(t > 4, -value, value)


def wave_sums(q_ref, rp_ref, table_ref, out_ref, weights_ref):
    groups = weights_ref.shape[1] // 16

    @pl.when(pl.program_id(0) == 0)
    def _():
        lane = lax.broadcasted_iota(jnp.int32, (16, 256), 1)
        row = lax.broadcasted_iota(jnp.int32, (16, 256), 0)
        spread = jnp.where((lane & 15) == row, 1.0, 0.0).astype(jnp.bfloat16)
        vectors = jnp.dot(
            rp_ref[...].astype(jnp.float32).astype(jnp.bfloat16),
            spread,
            preferred_element_type=jnp.float32,
        ).astype(jnp.int32)
        own = (lane >> 4) == row
        for q in range(2):
            n = (
                q_ref[q, 0] * vectors[0:1]
                + q_ref[q, 1] * vectors[1:2]
                + q_ref[q, 2] * vectors[2:3]
            )
            for part, value in enumerate((cosine(n), cosine(n - 4))):
                high = value.astype(jnp.bfloat16).astype(jnp.float32)
                for fine, piece in enumerate((high, value - high)):
                    at = 64 * fine + 32 * part + 16 * q
                    block = jnp.where(own, jnp.broadcast_to(piece, (16, 256)), 0.0)
                    weights_ref[at : at + 16, :] = block.astype(jnp.bfloat16)

    y = jnp.dot(weights_ref[...], table_ref[...], preferred_element_type=jnp.float32)
    y = y[:64] + y[64:]
    by_cos, by_sin = y[:32], y[32:]
    real = by_cos[:, :512] - by_sin[:, 512:]
    imag = by_sin[:, :512] + by_cos[:, 512:]
    low = lax.broadcasted_iota(jnp.int32, (16, LANES), 1) < HALF
    for q in range(2):
        for b in range(4):
            re = real[16 * q : 16 * q + 16, LANES * b : LANES * (b + 1)]
            im = imag[16 * q : 16 * q + 16, LANES * b : LANES * (b + 1)]
            first = jnp.where(low, re, pltpu.roll(im, HALF, 1))
            second = jnp.where(low, pltpu.roll(re, HALF, 1), im)
            out_ref[8 * q + 2 * b] = first.astype(out_ref.dtype)
            out_ref[8 * q + 2 * b + 1] = second.astype(out_ref.dtype)


def add_parts(parts_ref, out_ref):
    total = parts_ref[0].astype(jnp.float32)
    for r in range(1, parts_ref.shape[0]):
        total = total + parts_ref[r].astype(jnp.float32)
    high = total.astype(jnp.bfloat16)
    low = (total - high.astype(jnp.float32)).astype(jnp.bfloat16)
    for a in range(out_ref.shape[0]):
        out_ref[a, 0] = high
        out_ref[a, 1] = low


def bloch(mid_ref, k_ref, re_ref, out_ref, phase_ref):
    k = k_ref[...].astype(jnp.float32).astype(jnp.bfloat16)
    re = re_ref[...].astype(jnp.float32).astype(jnp.bfloat16)
    n = lax.dot_general(k, re, (((0,), (0,)), ((), ())), preferred_element_type=jnp.float32)
    n = n.astype(jnp.int32)
    phase_ref[:, :512] = cosine(n).astype(jnp.bfloat16)
    phase_ref[:, 512:] = cosine(n - 4).astype(jnp.bfloat16)
    low = lax.broadcasted_iota(jnp.int32, (512, LANES), 1) < HALF
    straight, turned = [], []
    for piece in range(2):
        x = mid_ref[:, piece].reshape(512, LANES).astype(jnp.float32)
        rolled = pltpu.roll(x, HALF, 1)
        straight.append(x)
        turned.append(jnp.where(low, -rolled, rolled))
    with_cos = jnp.concatenate(straight, axis=1).astype(jnp.bfloat16)
    with_sin = jnp.concatenate(turned, axis=1).astype(jnp.bfloat16)
    out = jnp.dot(phase_ref[:, :512], with_cos, preferred_element_type=jnp.float32)
    out = out + jnp.dot(phase_ref[:, 512:], with_sin, preferred_element_type=jnp.float32)
    out_ref[...] = out[:, :LANES] + out[:, LANES:]


def place(pieces_ref, out_ref):
    low = lax.broadcasted_iota(jnp.int32, (32, LANES), 1) < HALF
    for pair in range(8):
        x0 = pieces_ref[2 * pair].astype(jnp.float32)
        x1 = pieces_ref[2 * pair + 1].astype(jnp.float32)
        at = LANES * pair
        out_ref[:, at : at + LANES] = jnp.where(low, x0, pltpu.roll(x1, HALF, 1))
        out_ref[:, 1024 + at : 1024 + at + LANES] = jnp.where(low, pltpu.roll(x0, HALF, 1), x1)


def exchanged(x, axis):
    x = lax.all_to_all(x, axis, 0, 0, tiled=True)
    return pltpu.with_memory_space_constraint(x, pltpu.VMEM)


def per_device(coupling_table, k_points, re_vectors, rp_vectors, q_points):
    vmem = pl.BlockSpec(memory_space=pltpu.VMEM)
    smem = pl.BlockSpec(memory_space=pltpu.SMEM)
    table = coupling_table.reshape(1024, 1024)
    parts = pl.pallas_call(
        wave_sums,
        grid=(4,),
        in_specs=[smem, vmem, pl.BlockSpec((256, 1024), lambda g: (g, 0))],
        out_specs=pl.BlockSpec((16, 16, LANES), lambda g: (0, g, 0)),
        out_shape=pltpu.VMEM((16, 64, LANES), jnp.bfloat16),
        scratch_shapes=[pltpu.VMEM((128, 256), jnp.bfloat16)],
        name="wave_sums",
    )(q_points.T, rp_vectors, table)
    parts = exchanged(parts, "rp")
    mid = pl.pallas_call(
        add_parts,
        in_specs=[vmem],
        out_specs=vmem,
        out_shape=pltpu.VMEM((8, 2, 64, LANES), jnp.bfloat16),
        name="add_parts",
    )(parts)
    mid = exchanged(mid, "ka")
    columns = pl.pallas_call(
        bloch,
        in_specs=[vmem, vmem, vmem],
        out_specs=vmem,
        out_shape=pltpu.VMEM((512, LANES), jnp.float32),
        scratch_shapes=[pltpu.VMEM((512, 1024), jnp.bfloat16)],
        name="bloch",
    )(mid, k_points, re_vectors)
    pieces = exchanged(columns.reshape(16, 32, LANES), "rp")
    return pl.pallas_call(
        place,
        in_specs=[vmem],
        out_specs=vmem,
        out_shape=jax.ShapeDtypeStruct((32, 2048), jnp.float32),
        name="place",
    )(pieces)


def solution(mesh):
    placed = (P("ka", "rp", None), P(None, "ka"), P(), P(None, "rp"), P())
    return jax.shard_map(
        per_device, mesh=mesh, in_specs=placed, out_specs=P(("ka", "rp"), None), check_vma=False
    )
```

```python
import math

import jax
import jax.numpy as jnp
from jax import lax
from jax.experimental import pallas as pl
from jax.experimental.pallas import tpu as pltpu
from jax.sharding import PartitionSpec as P

NKG = 16
LANES = 128
HALF = 64
CHUNKS = 4
ROWS = 1024 // CHUNKS
QUARTER = [math.cos(2.0 * math.pi * n / NKG) for n in range(4)] + [0.0]
BITS = 14
SMALLEST = 2.0**-100


def cosine(n):
    m = n & (NKG - 1)
    t = jnp.minimum(m, NKG - m)
    u = jnp.minimum(t, 8 - t)
    value = jnp.full(n.shape, QUARTER[0], jnp.float32)
    for i in range(1, 5):
        value = jnp.where(u == i, jnp.float32(QUARTER[i]), value)
    return jnp.where(t > 4, -value, value)


def lower_half(rows):
    return lax.broadcasted_iota(jnp.int32, (rows, LANES), 1) < HALF


def exact(x):
    return x.astype(jnp.float32).astype(jnp.bfloat16)


def pack(x):
    most = jnp.maximum(jnp.max(jnp.abs(x), axis=0, keepdims=True), SMALLEST)
    exponent = jnp.ceil(jnp.log2(most))
    packed = jnp.round(x * jnp.exp2(BITS - exponent)).astype(jnp.int32).astype(jnp.int16)
    header = jnp.broadcast_to(exponent, (8, LANES)).astype(jnp.int32).astype(jnp.int16)
    return packed, header


def unpack(block):
    rows = block.shape[0] - 8
    exponent = block[rows:].astype(jnp.int32).astype(jnp.float32)
    unit = jnp.exp2(exponent - BITS)[0:1]
    return block[:rows].astype(jnp.int32).astype(jnp.float32) * unit


def fill_weights(q_ref, rp_ref, weights_ref):
    lane = lax.broadcasted_iota(jnp.int32, (16, 256), 1)
    row = lax.broadcasted_iota(jnp.int32, (16, 256), 0)
    spread = jnp.where((lane & 15) == row, 1.0, 0.0).astype(jnp.bfloat16)
    vectors = jnp.dot(exact(rp_ref[...]), spread, preferred_element_type=jnp.float32).astype(jnp.int32)
    own = (lane >> 4) == row
    for q in range(2):
        n = sum(q_ref[q, d] * vectors[d : d + 1] for d in range(3))
        for part, value in enumerate((cosine(n), cosine(n - 4))):
            high = value.astype(jnp.bfloat16).astype(jnp.float32)
            for fine, piece in enumerate((high, value - high)):
                at = 64 * fine + 32 * part + 16 * q
                block = jnp.where(own, jnp.broadcast_to(piece, (16, 256)), 0.0)
                weights_ref[at : at + 16, :] = block.astype(jnp.bfloat16)


def fill_phases(k_ref, re_ref, phase_ref):
    n = lax.dot_general(
        exact(k_ref[...]), exact(re_ref[...]), (((0,), (0,)), ((), ())), preferred_element_type=jnp.float32
    )
    n = n.astype(jnp.int32) & (NKG - 1)
    lane = lax.broadcasted_iota(jnp.int32, (8, LANES), 1)
    tables = [jnp.broadcast_to(cosine(lane - turn)[0:1], (512, LANES)) for turn in (0, 4)]
    for b in range(4):
        index = n[:, LANES * b : LANES * (b + 1)]
        for i, table in enumerate(tables):
            at = 512 * i + LANES * b
            phase_ref[:, at : at + LANES] = jnp.take_along_axis(table, index, axis=1).astype(jnp.bfloat16)


def wave_sums(table_hbm, k_hbm, re_hbm, rp_hbm, q_hbm, out_ref, phase_ref, table, k, re, rp, q, weights, sems):
    copies = [
        pltpu.make_async_copy(source, target, sems.at[CHUNKS + i])
        for i, (source, target) in enumerate(((k_hbm, k), (re_hbm, re), (rp_hbm, rp), (q_hbm, q)))
    ]
    chunks = [
        pltpu.make_async_copy(
            table_hbm.at[ROWS * g : ROWS * (g + 1)], table.at[ROWS * g : ROWS * (g + 1)], sems.at[g]
        )
        for g in range(CHUNKS)
    ]
    for copy in copies + chunks:
        copy.start()
    for copy in copies:
        copy.wait()
    fill_weights(q, rp, weights)
    fill_phases(k, re, phase_ref)
    low = lower_half(16)
    for g in range(CHUNKS):
        chunks[g].wait()
        y = jnp.dot(weights[...], table[ROWS * g : ROWS * (g + 1)], preferred_element_type=jnp.float32)
        y = y[:64] + y[64:]
        by_cos, by_sin = y[:32], y[32:]
        real = by_cos[:, :512] - by_sin[:, 512:]
        imag = by_sin[:, :512] + by_cos[:, 512:]
        rows = slice(16 * g, 16 * g + 16)
        for w in range(2):
            for b in range(4):
                re_part = real[16 * w : 16 * w + 16, LANES * b : LANES * (b + 1)]
                im_part = imag[16 * w : 16 * w + 16, LANES * b : LANES * (b + 1)]
                first = jnp.where(low, re_part, pltpu.roll(im_part, HALF, 1))
                second = jnp.where(low, pltpu.roll(re_part, HALF, 1), im_part)
                out_ref[8 * w + 2 * b, rows] = first.astype(out_ref.dtype)
                out_ref[8 * w + 2 * b + 1, rows] = second.astype(out_ref.dtype)


def add_parts(parts_ref, out_ref):
    total = parts_ref[0].astype(jnp.float32)
    for r in range(1, 16):
        total = total + parts_ref[r].astype(jnp.float32)
    packed, header = pack(total)
    for a in range(8):
        out_ref[a, :64] = packed
        out_ref[a, 64:] = header


def bloch(mid_ref, phase_ref, out_ref):
    straight, turned = [], []
    low = lower_half(64)
    for a in range(8):
        x = unpack(mid_ref[a])
        high = x.astype(jnp.bfloat16).astype(jnp.float32)
        row, turned_row = [], []
        for piece in (high, x - high):
            rolled = pltpu.roll(piece, HALF, 1)
            row.append(piece)
            turned_row.append(jnp.where(low, -rolled, rolled))
        straight.append(jnp.concatenate(row, axis=1).astype(jnp.bfloat16))
        turned.append(jnp.concatenate(turned_row, axis=1).astype(jnp.bfloat16))
    both = jnp.concatenate(straight + turned, axis=0)
    out = jnp.dot(phase_ref[...], both, preferred_element_type=jnp.float32)
    packed, header = pack(out[:, :LANES] + out[:, LANES:])
    for r in range(16):
        out_ref[r, :32] = packed[32 * r : 32 * r + 32]
        out_ref[r, 32:] = header


def place(pieces_ref, out_ref):
    low = lower_half(32)
    for pair in range(8):
        x0 = unpack(pieces_ref[2 * pair])
        x1 = unpack(pieces_ref[2 * pair + 1])
        at = LANES * pair
        out_ref[:, at : at + LANES] = jnp.where(low, x0, pltpu.roll(x1, HALF, 1))
        out_ref[:, 1024 + at : 1024 + at + LANES] = jnp.where(low, pltpu.roll(x0, HALF, 1), x1)


def in_vmem(x):
    return pltpu.with_memory_space_constraint(x, pltpu.VMEM)


def per_device(coupling_table, k_points, re_vectors, rp_vectors, q_points):
    vmem = pl.BlockSpec(memory_space=pltpu.VMEM)
    parts, phase = pl.pallas_call(
        wave_sums,
        in_specs=[pl.BlockSpec(memory_space=pl.ANY)] * 5,
        out_specs=[vmem, vmem],
        out_shape=[pltpu.VMEM((16, 64, LANES), jnp.bfloat16), pltpu.VMEM((512, 1024), jnp.bfloat16)],
        scratch_shapes=[
            pltpu.VMEM((1024, 1024), jnp.bfloat16),
            pltpu.VMEM((3, 512), jnp.int32),
            pltpu.VMEM((3, 512), jnp.int32),
            pltpu.VMEM((3, 16), jnp.int32),
            pltpu.SMEM((2, 3), jnp.int32),
            pltpu.VMEM((128, 256), jnp.bfloat16),
            pltpu.SemaphoreType.DMA((CHUNKS + 4,)),
        ],
        name="wave_sums",
    )(coupling_table.reshape(1024, 1024), k_points, re_vectors, rp_vectors, q_points.T)
    parts = lax.all_to_all(parts, "rp", 0, 0, tiled=True)
    mid = pl.pallas_call(
        add_parts,
        in_specs=[vmem],
        out_specs=vmem,
        out_shape=pltpu.VMEM((8, 72, LANES), jnp.int16),
        name="add_parts",
    )(in_vmem(parts))
    mid = lax.all_to_all(mid, "ka", 0, 0, tiled=True)
    pieces = pl.pallas_call(
        bloch,
        in_specs=[vmem, vmem],
        out_specs=vmem,
        out_shape=pltpu.VMEM((16, 40, LANES), jnp.int16),
        name="bloch",
    )(in_vmem(mid), in_vmem(phase))
    pieces = lax.all_to_all(pieces, "rp", 0, 0, tiled=True)
    return pl.pallas_call(
        place,
        in_specs=[vmem],
        out_specs=vmem,
        out_shape=jax.ShapeDtypeStruct((32, 2048), jnp.float32),
        name="place",
    )(in_vmem(pieces))


def solution(mesh):
    placed = (P("ka", "rp", None), P(None, "ka"), P(), P(None, "rp"), P())
    return jax.shard_map(
        per_device, mesh=mesh, in_specs=placed, out_specs=P(("ka", "rp"), None), check_vma=False
    )
```

```python
import math

import jax
import jax.numpy as jnp
from jax import lax
from jax.experimental import pallas as pl
from jax.experimental.pallas import tpu as pltpu
from jax.sharding import PartitionSpec as P

NKG = 16
LANES = 128
HALF = 64
CHUNKS = 1
ROWS = 1024 // CHUNKS
QUARTER = [math.cos(2.0 * math.pi * n / NKG) for n in range(4)] + [0.0]
BITS = 14
SMALLEST = 2.0**-100


def cosine(n):
    m = n & (NKG - 1)
    t = jnp.minimum(m, NKG - m)
    u = jnp.minimum(t, 8 - t)
    value = jnp.full(n.shape, QUARTER[0], jnp.float32)
    for i in range(1, 5):
        value = jnp.where(u == i, jnp.float32(QUARTER[i]), value)
    return jnp.where(t > 4, -value, value)


def lower_half(rows):
    return lax.broadcasted_iota(jnp.int32, (rows, LANES), 1) < HALF


def exact(x):
    return x.astype(jnp.float32).astype(jnp.bfloat16)


def pack(x):
    most = jnp.maximum(jnp.max(jnp.abs(x), axis=0, keepdims=True), SMALLEST)
    exponent = jnp.ceil(jnp.log2(most))
    packed = jnp.round(x * jnp.exp2(BITS - exponent)).astype(jnp.int32).astype(jnp.int16)
    header = jnp.broadcast_to(exponent, (8, LANES)).astype(jnp.int32).astype(jnp.int16)
    return packed, header


def unpack(block):
    rows = block.shape[0] - 8
    exponent = block[rows:].astype(jnp.int32).astype(jnp.float32)
    unit = jnp.exp2(exponent - BITS)[0:1]
    return block[:rows].astype(jnp.int32).astype(jnp.float32) * unit


def fill_weights(q_ref, rp_ref, weights_ref):
    lane = lax.broadcasted_iota(jnp.int32, (16, 256), 1)
    row = lax.broadcasted_iota(jnp.int32, (16, 256), 0)
    spread = jnp.where((lane & 15) == row, 1.0, 0.0).astype(jnp.bfloat16)
    vectors = jnp.dot(exact(rp_ref[...]), spread, preferred_element_type=jnp.float32).astype(jnp.int32)
    own = (lane >> 4) == row
    for q in range(2):
        n = sum(q_ref[q, d] * vectors[d : d + 1] for d in range(3))
        for part, value in enumerate((cosine(n), cosine(n - 4))):
            high = value.astype(jnp.bfloat16).astype(jnp.float32)
            for fine, piece in enumerate((high, value - high)):
                at = 64 * fine + 32 * part + 16 * q
                block = jnp.where(own, jnp.broadcast_to(piece, (16, 256)), 0.0)
                weights_ref[at : at + 16, :] = block.astype(jnp.bfloat16)


def fill_phases(k_ref, re_ref, phase_ref):
    n = lax.dot_general(
        exact(k_ref[...]), exact(re_ref[...]), (((0,), (0,)), ((), ())), preferred_element_type=jnp.float32
    )
    n = n.astype(jnp.int32) & (NKG - 1)
    lane = lax.broadcasted_iota(jnp.int32, (8, LANES), 1)
    tables = [jnp.broadcast_to(cosine(lane - turn)[0:1], (512, LANES)) for turn in (0, 4)]
    for b in range(4):
        index = n[:, LANES * b : LANES * (b + 1)]
        for i, table in enumerate(tables):
            at = 512 * i + LANES * b
            phase_ref[:, at : at + LANES] = jnp.take_along_axis(table, index, axis=1).astype(jnp.bfloat16)


def wave_sums(table_hbm, rp_hbm, q_hbm, keep_ref, send_ref, table, rp, q, weights, sems):
    small = [
        pltpu.make_async_copy(source, target, sems.at[CHUNKS + i])
        for i, (source, target) in enumerate(((rp_hbm, rp), (q_hbm, q)))
    ]
    chunks = [
        pltpu.make_async_copy(
            table_hbm.at[ROWS * g : ROWS * (g + 1)], table.at[ROWS * g : ROWS * (g + 1)], sems.at[g]
        )
        for g in range(CHUNKS)
    ]
    for copy in small + chunks:
        copy.start()
    for copy in small:
        copy.wait()
    fill_weights(q, rp, weights)
    low = lower_half(16)
    core0 = (lax.axis_index("rp") & 1) == 0
    for g in range(4):
        if (256 * g) % ROWS == 0:
            chunks[256 * g // ROWS].wait()
        y = jnp.dot(weights[...], table[256 * g : 256 * (g + 1)], preferred_element_type=jnp.float32)
        y = y[:64] + y[64:]
        by_cos, by_sin = y[:32], y[32:]
        real = by_cos[:, :512] - by_sin[:, 512:]
        imag = by_sin[:, :512] + by_cos[:, 512:]
        rows = slice(16 * g, 16 * g + 16)
        for w in range(2):
            for b in range(4):
                re = real[16 * w : 16 * w + 16, LANES * b : LANES * (b + 1)]
                im = imag[16 * w : 16 * w + 16, LANES * b : LANES * (b + 1)]
                first = jnp.where(low, re, pltpu.roll(im, HALF, 1))
                second = jnp.where(low, pltpu.roll(re, HALF, 1), im)
                keep_ref[4 * w + b, rows] = jnp.where(core0, first, second)
                send_ref[4 * w + b, rows] = jnp.where(core0, second, first)


def add_cores(keep_ref, got_ref, out_ref):
    out_ref[...] = (keep_ref[...] + got_ref[...]).astype(out_ref.dtype)


def add_parts(parts_ref, out_ref):
    total = parts_ref[0].astype(jnp.float32)
    for r in range(1, 8):
        total = total + parts_ref[r].astype(jnp.float32)
    packed, header = pack(total)
    for a in range(8):
        out_ref[a, :64] = packed
        out_ref[a, 64:] = header


def bloch(mid_ref, phase_ref, out_ref):
    straight, turned = [], []
    low = lower_half(64)
    for a in range(8):
        x = unpack(mid_ref[a])
        high = x.astype(jnp.bfloat16).astype(jnp.float32)
        row, turned_row = [], []
        for piece in (high, x - high):
            rolled = pltpu.roll(piece, HALF, 1)
            row.append(piece)
            turned_row.append(jnp.where(low, -rolled, rolled))
        straight.append(jnp.concatenate(row, axis=1).astype(jnp.bfloat16))
        turned.append(jnp.concatenate(turned_row, axis=1).astype(jnp.bfloat16))
    both = jnp.concatenate(straight + turned, axis=0)
    out = jnp.dot(phase_ref[...], both, preferred_element_type=jnp.float32)
    packed, header = pack(out[:, :LANES] + out[:, LANES:])
    for r in range(16):
        out_ref[r, :32] = packed[32 * r : 32 * r + 32]
        out_ref[r, 32:] = header


def place(pieces_ref, out_ref):
    low = lower_half(32)
    for pair in range(8):
        x0 = unpack(pieces_ref[2 * pair])
        x1 = unpack(pieces_ref[2 * pair + 1])
        at = LANES * pair
        out_ref[:, at : at + LANES] = jnp.where(low, x0, pltpu.roll(x1, HALF, 1))
        out_ref[:, 1024 + at : 1024 + at + LANES] = jnp.where(low, pltpu.roll(x0, HALF, 1), x1)


def in_vmem(x):
    return pltpu.with_memory_space_constraint(x, pltpu.VMEM)


def per_device(coupling_table, k_points, re_vectors, rp_vectors, q_points):
    vmem = pl.BlockSpec(memory_space=pltpu.VMEM)
    same_core = [[2 * chip + core for chip in range(8)] for core in range(2)]
    keep, send = pl.pallas_call(
        wave_sums,
        in_specs=[pl.BlockSpec(memory_space=pl.ANY)] * 3,
        out_specs=[vmem, vmem],
        out_shape=[pltpu.VMEM((8, 64, LANES), jnp.float32)] * 2,
        scratch_shapes=[
            pltpu.VMEM((1024, 1024), jnp.bfloat16),
            pltpu.VMEM((3, 16), jnp.int32),
            pltpu.SMEM((2, 3), jnp.int32),
            pltpu.VMEM((128, 256), jnp.bfloat16),
            pltpu.SemaphoreType.DMA((CHUNKS + 2,)),
        ],
        name="wave_sums",
    )(coupling_table.reshape(1024, 1024), rp_vectors, q_points.T)
    got = lax.ppermute(send, "rp", [(i, i ^ 1) for i in range(16)])
    phase = pl.pallas_call(
        fill_phases,
        in_specs=[vmem, vmem],
        out_specs=vmem,
        out_shape=pltpu.VMEM((512, 1024), jnp.bfloat16),
        name="phases",
    )(in_vmem(k_points), in_vmem(re_vectors))
    got, phase = lax.optimization_barrier((got, phase))
    parts = pl.pallas_call(
        add_cores,
        in_specs=[vmem, vmem],
        out_specs=vmem,
        out_shape=pltpu.VMEM((8, 64, LANES), jnp.bfloat16),
        name="add_cores",
    )(in_vmem(keep), in_vmem(got))
    parts = lax.all_to_all(parts, "rp", 0, 0, axis_index_groups=same_core, tiled=True)
    mid = pl.pallas_call(
        add_parts,
        in_specs=[vmem],
        out_specs=vmem,
        out_shape=pltpu.VMEM((8, 72, LANES), jnp.int16),
        name="add_parts",
    )(in_vmem(parts))
    mid = lax.all_to_all(mid, "ka", 0, 0, tiled=True)
    pieces = pl.pallas_call(
        bloch,
        in_specs=[vmem, vmem],
        out_specs=vmem,
        out_shape=pltpu.VMEM((16, 40, LANES), jnp.int16),
        name="bloch",
    )(in_vmem(mid), in_vmem(phase))
    pieces = lax.all_to_all(pieces, "rp", 0, 0, tiled=True)
    return pl.pallas_call(
        place,
        in_specs=[vmem],
        out_specs=vmem,
        out_shape=jax.ShapeDtypeStruct((32, 2048), jnp.float32),
        name="place",
    )(in_vmem(pieces))


def solution(mesh):
    placed = (P("ka", "rp", None), P(None, "ka"), P(), P(None, "rp"), P())
    return jax.shard_map(
        per_device, mesh=mesh, in_specs=placed, out_specs=P(("ka", "rp"), None), check_vma=False
    )
```

```python
import math

import jax
import jax.numpy as jnp
from jax import lax
from jax.experimental import pallas as pl
from jax.experimental.pallas import tpu as pltpu
from jax.sharding import PartitionSpec as P

NKG = 16
LANES = 128
HALF = 64
CHUNKS = 1
ROWS = 1024 // CHUNKS
QUARTER = [math.cos(2.0 * math.pi * n / NKG) for n in range(4)] + [0.0]
BITS = 14
SMALLEST = 2.0**-100


def cosine(n):
    m = n & (NKG - 1)
    t = jnp.minimum(m, NKG - m)
    u = jnp.minimum(t, 8 - t)
    value = jnp.full(n.shape, QUARTER[0], jnp.float32)
    for i in range(1, 5):
        value = jnp.where(u == i, jnp.float32(QUARTER[i]), value)
    return jnp.where(t > 4, -value, value)


def lower_half(rows):
    return lax.broadcasted_iota(jnp.int32, (rows, LANES), 1) < HALF


def exact(x):
    return x.astype(jnp.float32).astype(jnp.bfloat16)


def pack(x):
    most = jnp.maximum(jnp.max(jnp.abs(x), axis=0, keepdims=True), SMALLEST)
    exponent = jnp.ceil(jnp.log2(most))
    packed = jnp.round(x * jnp.exp2(BITS - exponent)).astype(jnp.int32).astype(jnp.int16)
    header = jnp.broadcast_to(exponent, (8, LANES)).astype(jnp.int32).astype(jnp.int16)
    return packed, header


def unpack(block):
    rows = block.shape[0] - 8
    exponent = block[rows:].astype(jnp.int32).astype(jnp.float32)
    unit = jnp.exp2(exponent - BITS)[0:1]
    return block[:rows].astype(jnp.int32).astype(jnp.float32) * unit


def fill_weights(q_ref, rp_ref, weights_ref):
    lane = lax.broadcasted_iota(jnp.int32, (16, 256), 1)
    row = lax.broadcasted_iota(jnp.int32, (16, 256), 0)
    spread = jnp.where((lane & 15) == row, 1.0, 0.0).astype(jnp.bfloat16)
    vectors = jnp.dot(exact(rp_ref[...]), spread, preferred_element_type=jnp.float32).astype(jnp.int32)
    own = (lane >> 4) == row
    for q in range(2):
        n = sum(q_ref[q, d] * vectors[d : d + 1] for d in range(3))
        for part, value in enumerate((cosine(n), cosine(n - 4))):
            high = value.astype(jnp.bfloat16).astype(jnp.float32)
            for fine, piece in enumerate((high, value - high)):
                at = 64 * fine + 32 * part + 16 * q
                block = jnp.where(own, jnp.broadcast_to(piece, (16, 256)), 0.0)
                weights_ref[at : at + 16, :] = block.astype(jnp.bfloat16)


def fill_phases(k_ref, re_ref, phase_ref):
    n = lax.dot_general(
        exact(k_ref[...]), exact(re_ref[...]), (((0,), (0,)), ((), ())), preferred_element_type=jnp.float32
    )
    n = n.astype(jnp.int32) & (NKG - 1)
    lane = lax.broadcasted_iota(jnp.int32, (8, LANES), 1)
    tables = [jnp.broadcast_to(cosine(lane - turn)[0:1], (512, LANES)) for turn in (0, 4)]
    for b in range(4):
        index = n[:, LANES * b : LANES * (b + 1)]
        for i, table in enumerate(tables):
            at = 512 * i + LANES * b
            phase_ref[:, at : at + LANES] = jnp.take_along_axis(table, index, axis=1).astype(jnp.bfloat16)


def wave_sums(table_hbm, k_hbm, re_hbm, rp_hbm, q_hbm, out_ref, phase_ref, table, k, re, rp, q, weights, sems):
    copies = [
        pltpu.make_async_copy(source, target, sems.at[CHUNKS + i])
        for i, (source, target) in enumerate(((k_hbm, k), (re_hbm, re), (rp_hbm, rp), (q_hbm, q)))
    ]
    chunks = [
        pltpu.make_async_copy(
            table_hbm.at[ROWS * g : ROWS * (g + 1)], table.at[ROWS * g : ROWS * (g + 1)], sems.at[g]
        )
        for g in range(CHUNKS)
    ]
    for copy in copies + chunks:
        copy.start()
    for copy in copies:
        copy.wait()
    fill_weights(q, rp, weights)
    fill_phases(k, re, phase_ref)
    low = lower_half(16)
    for g in range(4):
        if (256 * g) % ROWS == 0:
            chunks[256 * g // ROWS].wait()
        y = jnp.dot(weights[...], table[256 * g : 256 * (g + 1)], preferred_element_type=jnp.float32)
        y = y[:64] + y[64:]
        by_cos, by_sin = y[:32], y[32:]
        real = by_cos[:, :512] - by_sin[:, 512:]
        imag = by_sin[:, :512] + by_cos[:, 512:]
        rows = slice(16 * g, 16 * g + 16)
        for w in range(2):
            for b in range(4):
                re_part = real[16 * w : 16 * w + 16, LANES * b : LANES * (b + 1)]
                im_part = imag[16 * w : 16 * w + 16, LANES * b : LANES * (b + 1)]
                first = jnp.where(low, re_part, pltpu.roll(im_part, HALF, 1))
                second = jnp.where(low, pltpu.roll(re_part, HALF, 1), im_part)
                out_ref[8 * w + 2 * b, rows] = first.astype(out_ref.dtype)
                out_ref[8 * w + 2 * b + 1, rows] = second.astype(out_ref.dtype)


def add_parts(parts_ref, out_ref):
    total = parts_ref[0].astype(jnp.float32)
    for r in range(1, 16):
        total = total + parts_ref[r].astype(jnp.float32)
    packed, header = pack(total)
    for a in range(8):
        out_ref[a, :64] = packed
        out_ref[a, 64:] = header


def bloch(mid_ref, phase_ref, out_ref):
    straight, turned = [], []
    low = lower_half(64)
    for a in range(8):
        x = unpack(mid_ref[a])
        high = x.astype(jnp.bfloat16).astype(jnp.float32)
        row, turned_row = [], []
        for piece in (high, x - high):
            rolled = pltpu.roll(piece, HALF, 1)
            row.append(piece)
            turned_row.append(jnp.where(low, -rolled, rolled))
        straight.append(jnp.concatenate(row, axis=1).astype(jnp.bfloat16))
        turned.append(jnp.concatenate(turned_row, axis=1).astype(jnp.bfloat16))
    both = jnp.concatenate(straight + turned, axis=0)
    out = jnp.dot(phase_ref[...], both, preferred_element_type=jnp.float32)
    packed, header = pack(out[:, :LANES] + out[:, LANES:])
    for r in range(16):
        out_ref[r, :32] = packed[32 * r : 32 * r + 32]
        out_ref[r, 32:] = header


def place(pieces_ref, out_ref):
    low = lower_half(32)
    for pair in range(8):
        x0 = unpack(pieces_ref[2 * pair])
        x1 = unpack(pieces_ref[2 * pair + 1])
        at = LANES * pair
        out_ref[:, at : at + LANES] = jnp.where(low, x0, pltpu.roll(x1, HALF, 1))
        out_ref[:, 1024 + at : 1024 + at + LANES] = jnp.where(low, pltpu.roll(x0, HALF, 1), x1)


def in_vmem(x):
    return pltpu.with_memory_space_constraint(x, pltpu.VMEM)


def per_device(coupling_table, k_points, re_vectors, rp_vectors, q_points):
    vmem = pl.BlockSpec(memory_space=pltpu.VMEM)
    parts, phase = pl.pallas_call(
        wave_sums,
        in_specs=[pl.BlockSpec(memory_space=pl.ANY)] * 5,
        out_specs=[vmem, vmem],
        out_shape=[pltpu.VMEM((16, 64, LANES), jnp.bfloat16), pltpu.VMEM((512, 1024), jnp.bfloat16)],
        scratch_shapes=[
            pltpu.VMEM((1024, 1024), jnp.bfloat16),
            pltpu.VMEM((3, 512), jnp.int32),
            pltpu.VMEM((3, 512), jnp.int32),
            pltpu.VMEM((3, 16), jnp.int32),
            pltpu.SMEM((2, 3), jnp.int32),
            pltpu.VMEM((128, 256), jnp.bfloat16),
            pltpu.SemaphoreType.DMA((CHUNKS + 4,)),
        ],
        name="wave_sums",
    )(coupling_table.reshape(1024, 1024), k_points, re_vectors, rp_vectors, q_points.T)
    parts = lax.all_to_all(parts, "rp", 0, 0, tiled=True)
    mid = pl.pallas_call(
        add_parts,
        in_specs=[vmem],
        out_specs=vmem,
        out_shape=pltpu.VMEM((8, 72, LANES), jnp.int16),
        name="add_parts",
    )(in_vmem(parts))
    mid = lax.all_to_all(mid, "ka", 0, 0, tiled=True)
    pieces = pl.pallas_call(
        bloch,
        in_specs=[vmem, vmem],
        out_specs=vmem,
        out_shape=pltpu.VMEM((16, 40, LANES), jnp.int16),
        name="bloch",
    )(in_vmem(mid), in_vmem(phase))
    pieces = lax.all_to_all(pieces, "rp", 0, 0, tiled=True)
    return pl.pallas_call(
        place,
        in_specs=[vmem],
        out_specs=vmem,
        out_shape=jax.ShapeDtypeStruct((32, 2048), jnp.float32),
        name="place",
    )(in_vmem(pieces))


def solution(mesh):
    placed = (P("ka", "rp", None), P(None, "ka"), P(), P(None, "rp"), P())
    return jax.shard_map(
        per_device, mesh=mesh, in_specs=placed, out_specs=P(("ka", "rp"), None), check_vma=False
    )
```

```python
import math

import jax
import jax.numpy as jnp
from jax import lax
from jax.experimental import pallas as pl
from jax.experimental.pallas import tpu as pltpu
from jax.sharding import PartitionSpec as P

NKG = 16
LANES = 128
HALF = 64
CHUNKS = 1
ORDER = [4, 3, 15, 7, 10, 2, 1, 6, 0, 8, 9, 11, 12, 14, 13, 5]
PLACE = [ORDER.index(r) for r in range(16)]
ROWS = 1024 // CHUNKS
QUARTER = [math.cos(2.0 * math.pi * n / NKG) for n in range(4)] + [0.0]
BITS = 14
SMALLEST = 2.0**-100


def cosine(n):
    m = n & (NKG - 1)
    t = jnp.minimum(m, NKG - m)
    u = jnp.minimum(t, 8 - t)
    value = jnp.full(n.shape, QUARTER[0], jnp.float32)
    for i in range(1, 5):
        value = jnp.where(u == i, jnp.float32(QUARTER[i]), value)
    return jnp.where(t > 4, -value, value)


def lower_half(rows):
    return lax.broadcasted_iota(jnp.int32, (rows, LANES), 1) < HALF


def exact(x):
    return x.astype(jnp.float32).astype(jnp.bfloat16)


def pack(x):
    most = jnp.maximum(jnp.max(jnp.abs(x), axis=0, keepdims=True), SMALLEST)
    exponent = jnp.ceil(jnp.log2(most))
    packed = jnp.round(x * jnp.exp2(BITS - exponent)).astype(jnp.int32).astype(jnp.int16)
    header = jnp.broadcast_to(exponent, (8, LANES)).astype(jnp.int32).astype(jnp.int16)
    return packed, header


def unpack(block):
    rows = block.shape[0] - 8
    exponent = block[rows:].astype(jnp.int32).astype(jnp.float32)
    unit = jnp.exp2(exponent - BITS)[0:1]
    return block[:rows].astype(jnp.int32).astype(jnp.float32) * unit


def fill_weights(q_ref, rp_ref, weights_ref):
    lane = lax.broadcasted_iota(jnp.int32, (16, 256), 1)
    row = lax.broadcasted_iota(jnp.int32, (16, 256), 0)
    spread = jnp.where((lane & 15) == row, 1.0, 0.0).astype(jnp.bfloat16)
    vectors = jnp.dot(exact(rp_ref[...]), spread, preferred_element_type=jnp.float32).astype(jnp.int32)
    own = (lane >> 4) == row
    for q in range(2):
        n = sum(q_ref[q, d] * vectors[d : d + 1] for d in range(3))
        for part, value in enumerate((cosine(n), cosine(n - 4))):
            high = value.astype(jnp.bfloat16).astype(jnp.float32)
            for fine, piece in enumerate((high, value - high)):
                at = 64 * fine + 32 * part + 16 * q
                block = jnp.where(own, jnp.broadcast_to(piece, (16, 256)), 0.0)
                weights_ref[at : at + 16, :] = block.astype(jnp.bfloat16)


def fill_phases(k_ref, re_ref, phase_ref):
    n = lax.dot_general(
        exact(k_ref[...]), exact(re_ref[...]), (((0,), (0,)), ((), ())), preferred_element_type=jnp.float32
    )
    n = n.astype(jnp.int32) & (NKG - 1)
    lane = lax.broadcasted_iota(jnp.int32, (8, LANES), 1)
    tables = [jnp.broadcast_to(cosine(lane - turn)[0:1], (512, LANES)) for turn in (0, 4)]
    for b in range(4):
        index = n[:, LANES * b : LANES * (b + 1)]
        for i, table in enumerate(tables):
            at = 512 * i + LANES * b
            phase_ref[:, at : at + LANES] = jnp.take_along_axis(table, index, axis=1).astype(jnp.bfloat16)


def wave_sums(table_hbm, k_hbm, re_hbm, rp_hbm, q_hbm, out_ref, phase_ref, table, k, re, rp, q, weights, sems):
    copies = [
        pltpu.make_async_copy(source, target, sems.at[CHUNKS + i])
        for i, (source, target) in enumerate(((k_hbm, k), (re_hbm, re), (rp_hbm, rp), (q_hbm, q)))
    ]
    chunks = [
        pltpu.make_async_copy(
            table_hbm.at[ROWS * g : ROWS * (g + 1)], table.at[ROWS * g : ROWS * (g + 1)], sems.at[g]
        )
        for g in range(CHUNKS)
    ]
    for copy in copies + chunks:
        copy.start()
    for copy in copies:
        copy.wait()
    fill_weights(q, rp, weights)
    fill_phases(k, re, phase_ref)
    low = lower_half(16)
    for g in range(4):
        if (256 * g) % ROWS == 0:
            chunks[256 * g // ROWS].wait()
        y = jnp.dot(weights[...], table[256 * g : 256 * (g + 1)], preferred_element_type=jnp.float32)
        y = y[:64] + y[64:]
        by_cos, by_sin = y[:32], y[32:]
        real = by_cos[:, :512] - by_sin[:, 512:]
        imag = by_sin[:, :512] + by_cos[:, 512:]
        rows = slice(16 * g, 16 * g + 16)
        for w in range(2):
            for b in range(4):
                re_part = real[16 * w : 16 * w + 16, LANES * b : LANES * (b + 1)]
                im_part = imag[16 * w : 16 * w + 16, LANES * b : LANES * (b + 1)]
                first = jnp.where(low, re_part, pltpu.roll(im_part, HALF, 1))
                second = jnp.where(low, pltpu.roll(re_part, HALF, 1), im_part)
                out_ref[PLACE[8 * w + 2 * b], rows] = first.astype(out_ref.dtype)
                out_ref[PLACE[8 * w + 2 * b + 1], rows] = second.astype(out_ref.dtype)


def add_parts(parts_ref, out_ref):
    total = parts_ref[0].astype(jnp.float32)
    for r in range(1, 16):
        total = total + parts_ref[r].astype(jnp.float32)
    packed, header = pack(total)
    for a in range(8):
        out_ref[a, :64] = packed
        out_ref[a, 64:] = header


def bloch(mid_ref, phase_ref, out_ref):
    straight, turned = [], []
    low = lower_half(64)
    for a in range(8):
        x = unpack(mid_ref[a])
        high = x.astype(jnp.bfloat16).astype(jnp.float32)
        row, turned_row = [], []
        for piece in (high, x - high):
            rolled = pltpu.roll(piece, HALF, 1)
            row.append(piece)
            turned_row.append(jnp.where(low, -rolled, rolled))
        straight.append(jnp.concatenate(row, axis=1).astype(jnp.bfloat16))
        turned.append(jnp.concatenate(turned_row, axis=1).astype(jnp.bfloat16))
    both = jnp.concatenate(straight + turned, axis=0)
    out = jnp.dot(phase_ref[...], both, preferred_element_type=jnp.float32)
    packed, header = pack(out[:, :LANES] + out[:, LANES:])
    for r in range(16):
        out_ref[PLACE[r], :32] = packed[32 * r : 32 * r + 32]
        out_ref[PLACE[r], 32:] = header


def place(pieces_ref, out_ref):
    low = lower_half(32)
    for pair in range(8):
        x0 = unpack(pieces_ref[PLACE[2 * pair]])
        x1 = unpack(pieces_ref[PLACE[2 * pair + 1]])
        at = LANES * pair
        out_ref[:, at : at + LANES] = jnp.where(low, x0, pltpu.roll(x1, HALF, 1))
        out_ref[:, 1024 + at : 1024 + at + LANES] = jnp.where(low, pltpu.roll(x0, HALF, 1), x1)


def in_vmem(x):
    return pltpu.with_memory_space_constraint(x, pltpu.VMEM)


def per_device(coupling_table, k_points, re_vectors, rp_vectors, q_points):
    vmem = pl.BlockSpec(memory_space=pltpu.VMEM)
    parts, phase = pl.pallas_call(
        wave_sums,
        in_specs=[pl.BlockSpec(memory_space=pl.ANY)] * 5,
        out_specs=[vmem, vmem],
        out_shape=[pltpu.VMEM((16, 64, LANES), jnp.bfloat16), pltpu.VMEM((512, 1024), jnp.bfloat16)],
        scratch_shapes=[
            pltpu.VMEM((1024, 1024), jnp.bfloat16),
            pltpu.VMEM((3, 512), jnp.int32),
            pltpu.VMEM((3, 512), jnp.int32),
            pltpu.VMEM((3, 16), jnp.int32),
            pltpu.SMEM((2, 3), jnp.int32),
            pltpu.VMEM((128, 256), jnp.bfloat16),
            pltpu.SemaphoreType.DMA((CHUNKS + 4,)),
        ],
        name="wave_sums",
    )(coupling_table.reshape(1024, 1024), k_points, re_vectors, rp_vectors, q_points.T)
    parts = lax.all_to_all(parts, "rp", 0, 0, axis_index_groups=[ORDER], tiled=True)
    mid = pl.pallas_call(
        add_parts,
        in_specs=[vmem],
        out_specs=vmem,
        out_shape=pltpu.VMEM((8, 72, LANES), jnp.int16),
        name="add_parts",
    )(in_vmem(parts))
    mid = lax.all_to_all(mid, "ka", 0, 0, tiled=True)
    pieces = pl.pallas_call(
        bloch,
        in_specs=[vmem, vmem],
        out_specs=vmem,
        out_shape=pltpu.VMEM((16, 40, LANES), jnp.int16),
        name="bloch",
    )(in_vmem(mid), in_vmem(phase))
    pieces = lax.all_to_all(pieces, "rp", 0, 0, axis_index_groups=[ORDER], tiled=True)
    return pl.pallas_call(
        place,
        in_specs=[vmem],
        out_specs=vmem,
        out_shape=jax.ShapeDtypeStruct((32, 2048), jnp.float32),
        name="place",
    )(in_vmem(pieces))


def solution(mesh):
    placed = (P("ka", "rp", None), P(None, "ka"), P(), P(None, "rp"), P())
    return jax.shard_map(
        per_device, mesh=mesh, in_specs=placed, out_specs=P(("ka", "rp"), None), check_vma=False
    )
```

```python
import math

import jax
import jax.numpy as jnp
from jax import lax
from jax.experimental import pallas as pl
from jax.experimental.pallas import tpu as pltpu
from jax.sharding import PartitionSpec as P

NKG = 16
LANES = 128
HALF = 64
CHUNKS = 1
ROWS = 1024 // CHUNKS
ORDER1 = [5, 11, 9, 3, 12, 10, 8, 6, 14, 2, 7, 15, 13, 4, 0, 1]
ORDER2 = [5, 1, 2, 0, 6, 3, 4, 7]
ORDER3 = [4, 3, 15, 7, 10, 2, 1, 6, 0, 8, 9, 11, 12, 14, 13, 5]
PLACE1 = [ORDER1.index(r) for r in range(16)]
PLACE2 = [ORDER2.index(a) for a in range(8)]
PLACE3 = [ORDER3.index(r) for r in range(16)]
QUARTER = [math.cos(2.0 * math.pi * n / NKG) for n in range(4)] + [0.0]
BITS = 14
SMALLEST = 2.0**-100


def cosine(n):
    m = n & (NKG - 1)
    t = jnp.minimum(m, NKG - m)
    u = jnp.minimum(t, 8 - t)
    value = jnp.full(n.shape, QUARTER[0], jnp.float32)
    for i in range(1, 5):
        value = jnp.where(u == i, jnp.float32(QUARTER[i]), value)
    return jnp.where(t > 4, -value, value)


def lower_half(rows):
    return lax.broadcasted_iota(jnp.int32, (rows, LANES), 1) < HALF


def exact(x):
    return x.astype(jnp.float32).astype(jnp.bfloat16)


def pack(x):
    most = jnp.maximum(jnp.max(jnp.abs(x), axis=0, keepdims=True), SMALLEST)
    exponent = jnp.ceil(jnp.log2(most))
    packed = jnp.round(x * jnp.exp2(BITS - exponent)).astype(jnp.int32).astype(jnp.int16)
    header = jnp.broadcast_to(exponent, (8, LANES)).astype(jnp.int32).astype(jnp.int16)
    return packed, header


def unpack(block):
    rows = block.shape[0] - 8
    exponent = block[rows:].astype(jnp.int32).astype(jnp.float32)
    unit = jnp.exp2(exponent - BITS)[0:1]
    return block[:rows].astype(jnp.int32).astype(jnp.float32) * unit


def fill_weights(q_ref, rp_ref, weights_ref):
    lane = lax.broadcasted_iota(jnp.int32, (16, 256), 1)
    row = lax.broadcasted_iota(jnp.int32, (16, 256), 0)
    spread = jnp.where((lane & 15) == row, 1.0, 0.0).astype(jnp.bfloat16)
    vectors = jnp.dot(exact(rp_ref[...]), spread, preferred_element_type=jnp.float32).astype(jnp.int32)
    own = (lane >> 4) == row
    for q in range(2):
        n = sum(q_ref[q, d] * vectors[d : d + 1] for d in range(3))
        for part, value in enumerate((cosine(n), cosine(n - 4))):
            high = value.astype(jnp.bfloat16).astype(jnp.float32)
            for fine, piece in enumerate((high, value - high)):
                at = 64 * fine + 32 * part + 16 * q
                block = jnp.where(own, jnp.broadcast_to(piece, (16, 256)), 0.0)
                weights_ref[at : at + 16, :] = block.astype(jnp.bfloat16)


def fill_phases(k_ref, re_ref, phase_ref):
    n = lax.dot_general(
        exact(k_ref[...]), exact(re_ref[...]), (((0,), (0,)), ((), ())), preferred_element_type=jnp.float32
    )
    n = n.astype(jnp.int32) & (NKG - 1)
    lane = lax.broadcasted_iota(jnp.int32, (8, LANES), 1)
    tables = [jnp.broadcast_to(cosine(lane - turn)[0:1], (512, LANES)) for turn in (0, 4)]
    for b in range(4):
        index = n[:, LANES * b : LANES * (b + 1)]
        for i, table in enumerate(tables):
            at = 512 * i + LANES * b
            phase_ref[:, at : at + LANES] = jnp.take_along_axis(table, index, axis=1).astype(jnp.bfloat16)


def wave_sums(table_hbm, k_hbm, re_hbm, rp_hbm, q_hbm, out_ref, phase_ref, table, k, re, rp, q, weights, sems):
    copies = [
        pltpu.make_async_copy(source, target, sems.at[CHUNKS + i])
        for i, (source, target) in enumerate(((k_hbm, k), (re_hbm, re), (rp_hbm, rp), (q_hbm, q)))
    ]
    chunks = [
        pltpu.make_async_copy(
            table_hbm.at[ROWS * g : ROWS * (g + 1)], table.at[ROWS * g : ROWS * (g + 1)], sems.at[g]
        )
        for g in range(CHUNKS)
    ]
    for copy in copies + chunks:
        copy.start()
    for copy in copies:
        copy.wait()
    fill_weights(q, rp, weights)
    fill_phases(k, re, phase_ref)
    low = lower_half(16)
    for g in range(4):
        if (256 * g) % ROWS == 0:
            chunks[256 * g // ROWS].wait()
        y = jnp.dot(weights[...], table[256 * g : 256 * (g + 1)], preferred_element_type=jnp.float32)
        y = y[:64] + y[64:]
        by_cos, by_sin = y[:32], y[32:]
        real = by_cos[:, :512] - by_sin[:, 512:]
        imag = by_sin[:, :512] + by_cos[:, 512:]
        rows = slice(16 * g, 16 * g + 16)
        for w in range(2):
            for b in range(4):
                re_part = real[16 * w : 16 * w + 16, LANES * b : LANES * (b + 1)]
                im_part = imag[16 * w : 16 * w + 16, LANES * b : LANES * (b + 1)]
                first = jnp.where(low, re_part, pltpu.roll(im_part, HALF, 1))
                second = jnp.where(low, pltpu.roll(re_part, HALF, 1), im_part)
                out_ref[PLACE1[8 * w + 2 * b], rows] = first.astype(out_ref.dtype)
                out_ref[PLACE1[8 * w + 2 * b + 1], rows] = second.astype(out_ref.dtype)


def add_parts(parts_ref, out_ref):
    total = parts_ref[0].astype(jnp.float32)
    for r in range(1, 16):
        total = total + parts_ref[r].astype(jnp.float32)
    packed, header = pack(total)
    for a in range(8):
        out_ref[a, :64] = packed
        out_ref[a, 64:] = header


def bloch(mid_ref, phase_ref, out_ref):
    straight, turned = [], []
    low = lower_half(64)
    for a in range(8):
        x = unpack(mid_ref[PLACE2[a]])
        high = x.astype(jnp.bfloat16).astype(jnp.float32)
        row, turned_row = [], []
        for piece in (high, x - high):
            rolled = pltpu.roll(piece, HALF, 1)
            row.append(piece)
            turned_row.append(jnp.where(low, -rolled, rolled))
        straight.append(jnp.concatenate(row, axis=1).astype(jnp.bfloat16))
        turned.append(jnp.concatenate(turned_row, axis=1).astype(jnp.bfloat16))
    both = jnp.concatenate(straight + turned, axis=0)
    out = jnp.dot(phase_ref[...], both, preferred_element_type=jnp.float32)
    packed, header = pack(out[:, :LANES] + out[:, LANES:])
    for r in range(16):
        out_ref[PLACE3[r], :32] = packed[32 * r : 32 * r + 32]
        out_ref[PLACE3[r], 32:] = header


def place(pieces_ref, out_ref):
    low = lower_half(32)
    for pair in range(8):
        x0 = unpack(pieces_ref[PLACE3[2 * pair]])
        x1 = unpack(pieces_ref[PLACE3[2 * pair + 1]])
        at = LANES * pair
        out_ref[:, at : at + LANES] = jnp.where(low, x0, pltpu.roll(x1, HALF, 1))
        out_ref[:, 1024 + at : 1024 + at + LANES] = jnp.where(low, pltpu.roll(x0, HALF, 1), x1)


def in_vmem(x):
    return pltpu.with_memory_space_constraint(x, pltpu.VMEM)


def per_device(coupling_table, k_points, re_vectors, rp_vectors, q_points):
    vmem = pl.BlockSpec(memory_space=pltpu.VMEM)
    parts, phase = pl.pallas_call(
        wave_sums,
        in_specs=[pl.BlockSpec(memory_space=pl.ANY)] * 5,
        out_specs=[vmem, vmem],
        out_shape=[pltpu.VMEM((16, 64, LANES), jnp.bfloat16), pltpu.VMEM((512, 1024), jnp.bfloat16)],
        scratch_shapes=[
            pltpu.VMEM((1024, 1024), jnp.bfloat16),
            pltpu.VMEM((3, 512), jnp.int32),
            pltpu.VMEM((3, 512), jnp.int32),
            pltpu.VMEM((3, 16), jnp.int32),
            pltpu.SMEM((2, 3), jnp.int32),
            pltpu.VMEM((128, 256), jnp.bfloat16),
            pltpu.SemaphoreType.DMA((CHUNKS + 4,)),
        ],
        name="wave_sums",
    )(coupling_table.reshape(1024, 1024), k_points, re_vectors, rp_vectors, q_points.T)
    parts = lax.all_to_all(parts, "rp", 0, 0, axis_index_groups=[ORDER1], tiled=True)
    mid = pl.pallas_call(
        add_parts,
        in_specs=[vmem],
        out_specs=vmem,
        out_shape=pltpu.VMEM((8, 72, LANES), jnp.int16),
        name="add_parts",
    )(in_vmem(parts))
    mid = lax.all_to_all(mid, "ka", 0, 0, axis_index_groups=[ORDER2], tiled=True)
    pieces = pl.pallas_call(
        bloch,
        in_specs=[vmem, vmem],
        out_specs=vmem,
        out_shape=pltpu.VMEM((16, 40, LANES), jnp.int16),
        name="bloch",
    )(in_vmem(mid), in_vmem(phase))
    pieces = lax.all_to_all(pieces, "rp", 0, 0, axis_index_groups=[ORDER3], tiled=True)
    return pl.pallas_call(
        place,
        in_specs=[vmem],
        out_specs=vmem,
        out_shape=jax.ShapeDtypeStruct((32, 2048), jnp.float32),
        name="place",
    )(in_vmem(pieces))


def solution(mesh):
    placed = (P("ka", "rp", None), P(None, "ka"), P(), P(None, "rp"), P())
    return jax.shard_map(
        per_device, mesh=mesh, in_specs=placed, out_specs=P(("ka", "rp"), None), check_vma=False
    )
```

```python
import math

import jax
import jax.numpy as jnp
from jax import lax
from jax.experimental import pallas as pl
from jax.experimental.pallas import tpu as pltpu
from jax.sharding import PartitionSpec as P

NKG = 16
LANES = 128
HALF = 64
CHUNKS = 1
ROWS = 1024 // CHUNKS
ORDER1 = [13, 12, 15, 14, 11, 10, 9, 8, 5, 4, 7, 6, 3, 2, 1, 0]
ORDER2 = [5, 4, 3, 2, 7, 6, 1, 0]
ORDER3 = [13, 5, 12, 4, 15, 7, 14, 6, 11, 3, 10, 2, 9, 1, 8, 0]
PLACE1 = [ORDER1.index(r) for r in range(16)]
PLACE2 = [ORDER2.index(a) for a in range(8)]
PLACE3 = [ORDER3.index(r) for r in range(16)]
QUARTER = [math.cos(2.0 * math.pi * n / NKG) for n in range(4)] + [0.0]
BITS = 14
SMALLEST = 2.0**-100


def cosine(n):
    m = n & (NKG - 1)
    t = jnp.minimum(m, NKG - m)
    u = jnp.minimum(t, 8 - t)
    value = jnp.full(n.shape, QUARTER[0], jnp.float32)
    for i in range(1, 5):
        value = jnp.where(u == i, jnp.float32(QUARTER[i]), value)
    return jnp.where(t > 4, -value, value)


def lower_half(rows):
    return lax.broadcasted_iota(jnp.int32, (rows, LANES), 1) < HALF


def exact(x):
    return x.astype(jnp.float32).astype(jnp.bfloat16)


def pack(x):
    most = jnp.maximum(jnp.max(jnp.abs(x), axis=0, keepdims=True), SMALLEST)
    exponent = jnp.ceil(jnp.log2(most))
    packed = jnp.round(x * jnp.exp2(BITS - exponent)).astype(jnp.int32).astype(jnp.int16)
    header = jnp.broadcast_to(exponent, (8, LANES)).astype(jnp.int32).astype(jnp.int16)
    return packed, header


def unpack(block):
    rows = block.shape[0] - 8
    exponent = block[rows:].astype(jnp.int32).astype(jnp.float32)
    unit = jnp.exp2(exponent - BITS)[0:1]
    return block[:rows].astype(jnp.int32).astype(jnp.float32) * unit


def fill_weights(q_ref, rp_ref, weights_ref):
    lane = lax.broadcasted_iota(jnp.int32, (16, 256), 1)
    row = lax.broadcasted_iota(jnp.int32, (16, 256), 0)
    spread = jnp.where((lane & 15) == row, 1.0, 0.0).astype(jnp.bfloat16)
    vectors = jnp.dot(exact(rp_ref[...]), spread, preferred_element_type=jnp.float32).astype(jnp.int32)
    own = (lane >> 4) == row
    for q in range(2):
        n = sum(q_ref[q, d] * vectors[d : d + 1] for d in range(3))
        for part, value in enumerate((cosine(n), cosine(n - 4))):
            high = value.astype(jnp.bfloat16).astype(jnp.float32)
            for fine, piece in enumerate((high, value - high)):
                at = 64 * fine + 32 * part + 16 * q
                block = jnp.where(own, jnp.broadcast_to(piece, (16, 256)), 0.0)
                weights_ref[at : at + 16, :] = block.astype(jnp.bfloat16)


def fill_phases(k_ref, re_ref, phase_ref):
    n = lax.dot_general(
        exact(k_ref[...]), exact(re_ref[...]), (((0,), (0,)), ((), ())), preferred_element_type=jnp.float32
    )
    n = n.astype(jnp.int32) & (NKG - 1)
    lane = lax.broadcasted_iota(jnp.int32, (8, LANES), 1)
    tables = [jnp.broadcast_to(cosine(lane - turn)[0:1], (512, LANES)) for turn in (0, 4)]
    for b in range(4):
        index = n[:, LANES * b : LANES * (b + 1)]
        for i, table in enumerate(tables):
            at = 512 * i + LANES * b
            phase_ref[:, at : at + LANES] = jnp.take_along_axis(table, index, axis=1).astype(jnp.bfloat16)


def wave_sums(table_hbm, k_hbm, re_hbm, rp_hbm, q_hbm, out_ref, phase_ref, table, k, re, rp, q, weights, sems):
    copies = [
        pltpu.make_async_copy(source, target, sems.at[CHUNKS + i])
        for i, (source, target) in enumerate(((k_hbm, k), (re_hbm, re), (rp_hbm, rp), (q_hbm, q)))
    ]
    chunks = [
        pltpu.make_async_copy(
            table_hbm.at[ROWS * g : ROWS * (g + 1)], table.at[ROWS * g : ROWS * (g + 1)], sems.at[g]
        )
        for g in range(CHUNKS)
    ]
    for copy in copies + chunks:
        copy.start()
    for copy in copies:
        copy.wait()
    fill_weights(q, rp, weights)
    fill_phases(k, re, phase_ref)
    low = lower_half(16)
    for g in range(4):
        if (256 * g) % ROWS == 0:
            chunks[256 * g // ROWS].wait()
        y = jnp.dot(weights[...], table[256 * g : 256 * (g + 1)], preferred_element_type=jnp.float32)
        y = y[:64] + y[64:]
        by_cos, by_sin = y[:32], y[32:]
        real = by_cos[:, :512] - by_sin[:, 512:]
        imag = by_sin[:, :512] + by_cos[:, 512:]
        rows = slice(16 * g, 16 * g + 16)
        for w in range(2):
            for b in range(4):
                re_part = real[16 * w : 16 * w + 16, LANES * b : LANES * (b + 1)]
                im_part = imag[16 * w : 16 * w + 16, LANES * b : LANES * (b + 1)]
                first = jnp.where(low, re_part, pltpu.roll(im_part, HALF, 1))
                second = jnp.where(low, pltpu.roll(re_part, HALF, 1), im_part)
                out_ref[PLACE1[8 * w + 2 * b], rows] = first.astype(out_ref.dtype)
                out_ref[PLACE1[8 * w + 2 * b + 1], rows] = second.astype(out_ref.dtype)


def add_parts(parts_ref, out_ref):
    total = parts_ref[0].astype(jnp.float32)
    for r in range(1, 16):
        total = total + parts_ref[r].astype(jnp.float32)
    packed, header = pack(total)
    for a in range(8):
        out_ref[a, :64] = packed
        out_ref[a, 64:] = header


def bloch(mid_ref, phase_ref, out_ref):
    straight, turned = [], []
    low = lower_half(64)
    for a in range(8):
        x = unpack(mid_ref[PLACE2[a]])
        high = x.astype(jnp.bfloat16).astype(jnp.float32)
        row, turned_row = [], []
        for piece in (high, x - high):
            rolled = pltpu.roll(piece, HALF, 1)
            row.append(piece)
            turned_row.append(jnp.where(low, -rolled, rolled))
        straight.append(jnp.concatenate(row, axis=1).astype(jnp.bfloat16))
        turned.append(jnp.concatenate(turned_row, axis=1).astype(jnp.bfloat16))
    both = jnp.concatenate(straight + turned, axis=0)
    out = jnp.dot(phase_ref[...], both, preferred_element_type=jnp.float32)
    packed, header = pack(out[:, :LANES] + out[:, LANES:])
    for r in range(16):
        out_ref[PLACE3[r], :32] = packed[32 * r : 32 * r + 32]
        out_ref[PLACE3[r], 32:] = header


def place(pieces_ref, out_ref):
    low = lower_half(32)
    for pair in range(8):
        x0 = unpack(pieces_ref[PLACE3[2 * pair]])
        x1 = unpack(pieces_ref[PLACE3[2 * pair + 1]])
        at = LANES * pair
        out_ref[:, at : at + LANES] = jnp.where(low, x0, pltpu.roll(x1, HALF, 1))
        out_ref[:, 1024 + at : 1024 + at + LANES] = jnp.where(low, pltpu.roll(x0, HALF, 1), x1)


def in_vmem(x):
    return pltpu.with_memory_space_constraint(x, pltpu.VMEM)


def per_device(coupling_table, k_points, re_vectors, rp_vectors, q_points):
    vmem = pl.BlockSpec(memory_space=pltpu.VMEM)
    parts, phase = pl.pallas_call(
        wave_sums,
        in_specs=[pl.BlockSpec(memory_space=pl.ANY)] * 5,
        out_specs=[vmem, vmem],
        out_shape=[pltpu.VMEM((16, 64, LANES), jnp.bfloat16), pltpu.VMEM((512, 1024), jnp.bfloat16)],
        scratch_shapes=[
            pltpu.VMEM((1024, 1024), jnp.bfloat16),
            pltpu.VMEM((3, 512), jnp.int32),
            pltpu.VMEM((3, 512), jnp.int32),
            pltpu.VMEM((3, 16), jnp.int32),
            pltpu.SMEM((2, 3), jnp.int32),
            pltpu.VMEM((128, 256), jnp.bfloat16),
            pltpu.SemaphoreType.DMA((CHUNKS + 4,)),
        ],
        name="wave_sums",
    )(coupling_table.reshape(1024, 1024), k_points, re_vectors, rp_vectors, q_points.T)
    parts = lax.all_to_all(parts, "rp", 0, 0, axis_index_groups=[ORDER1], tiled=True)
    mid = pl.pallas_call(
        add_parts,
        in_specs=[vmem],
        out_specs=vmem,
        out_shape=pltpu.VMEM((8, 72, LANES), jnp.int16),
        name="add_parts",
    )(in_vmem(parts))
    mid = lax.all_to_all(mid, "ka", 0, 0, axis_index_groups=[ORDER2], tiled=True)
    pieces = pl.pallas_call(
        bloch,
        in_specs=[vmem, vmem],
        out_specs=vmem,
        out_shape=pltpu.VMEM((16, 40, LANES), jnp.int16),
        name="bloch",
    )(in_vmem(mid), in_vmem(phase))
    pieces = lax.all_to_all(pieces, "rp", 0, 0, axis_index_groups=[ORDER3], tiled=True)
    return pl.pallas_call(
        place,
        in_specs=[vmem],
        out_specs=vmem,
        out_shape=jax.ShapeDtypeStruct((32, 2048), jnp.float32),
        name="place",
    )(in_vmem(pieces))


def solution(mesh):
    placed = (P("ka", "rp", None), P(None, "ka"), P(), P(None, "rp"), P())
    return jax.shard_map(
        per_device, mesh=mesh, in_specs=placed, out_specs=P(("ka", "rp"), None), check_vma=False
    )
```

```python
import math

import jax
import jax.numpy as jnp
from jax import lax
from jax.experimental import pallas as pl
from jax.experimental.pallas import tpu as pltpu
from jax.sharding import PartitionSpec as P

NKG = 16
LANES = 128
HALF = 64
CHUNKS = 1
ROWS = 1024 // CHUNKS
ORDER1 = [13, 12, 15, 14, 11, 10, 9, 8, 5, 2, 7, 6, 3, 4, 1, 0]
ORDER2 = [5, 4, 3, 2, 7, 6, 1, 0]
ORDER3 = [13, 5, 12, 4, 15, 7, 14, 6, 11, 3, 10, 2, 9, 1, 8, 0]
PLACE1 = [ORDER1.index(r) for r in range(16)]
PLACE2 = [ORDER2.index(a) for a in range(8)]
PLACE3 = [ORDER3.index(r) for r in range(16)]
QUARTER = [math.cos(2.0 * math.pi * n / NKG) for n in range(4)] + [0.0]
BITS = 14
SMALLEST = 2.0**-100


def cosine(n):
    m = n & (NKG - 1)
    t = jnp.minimum(m, NKG - m)
    u = jnp.minimum(t, 8 - t)
    value = jnp.full(n.shape, QUARTER[0], jnp.float32)
    for i in range(1, 5):
        value = jnp.where(u == i, jnp.float32(QUARTER[i]), value)
    return jnp.where(t > 4, -value, value)


def lower_half(rows):
    return lax.broadcasted_iota(jnp.int32, (rows, LANES), 1) < HALF


def exact(x):
    return x.astype(jnp.float32).astype(jnp.bfloat16)


def pack(x):
    most = jnp.maximum(jnp.max(jnp.abs(x), axis=0, keepdims=True), SMALLEST)
    exponent = jnp.ceil(jnp.log2(most))
    packed = jnp.round(x * jnp.exp2(BITS - exponent)).astype(jnp.int32).astype(jnp.int16)
    header = jnp.broadcast_to(exponent, (8, LANES)).astype(jnp.int32).astype(jnp.int16)
    return packed, header


def unpack(block):
    rows = block.shape[0] - 8
    exponent = block[rows:].astype(jnp.int32).astype(jnp.float32)
    unit = jnp.exp2(exponent - BITS)[0:1]
    return block[:rows].astype(jnp.int32).astype(jnp.float32) * unit


def fill_weights(q_ref, rp_ref, weights_ref):
    lane = lax.broadcasted_iota(jnp.int32, (16, 256), 1)
    row = lax.broadcasted_iota(jnp.int32, (16, 256), 0)
    spread = jnp.where((lane & 15) == row, 1.0, 0.0).astype(jnp.bfloat16)
    vectors = jnp.dot(exact(rp_ref[...]), spread, preferred_element_type=jnp.float32).astype(jnp.int32)
    own = (lane >> 4) == row
    for q in range(2):
        n = sum(q_ref[q, d] * vectors[d : d + 1] for d in range(3))
        for part, value in enumerate((cosine(n), cosine(n - 4))):
            high = value.astype(jnp.bfloat16).astype(jnp.float32)
            for fine, piece in enumerate((high, value - high)):
                at = 64 * fine + 32 * part + 16 * q
                block = jnp.where(own, jnp.broadcast_to(piece, (16, 256)), 0.0)
                weights_ref[at : at + 16, :] = block.astype(jnp.bfloat16)


def fill_phases(k_ref, re_ref, phase_ref):
    n = lax.dot_general(
        exact(k_ref[...]), exact(re_ref[...]), (((0,), (0,)), ((), ())), preferred_element_type=jnp.float32
    )
    n = n.astype(jnp.int32) & (NKG - 1)
    lane = lax.broadcasted_iota(jnp.int32, (8, LANES), 1)
    tables = [jnp.broadcast_to(cosine(lane - turn)[0:1], (512, LANES)) for turn in (0, 4)]
    for b in range(4):
        index = n[:, LANES * b : LANES * (b + 1)]
        for i, table in enumerate(tables):
            at = 512 * i + LANES * b
            phase_ref[:, at : at + LANES] = jnp.take_along_axis(table, index, axis=1).astype(jnp.bfloat16)


def wave_sums(table_hbm, k_hbm, re_hbm, rp_hbm, q_hbm, out_ref, phase_ref, table, k, re, rp, q, weights, sems):
    copies = [
        pltpu.make_async_copy(source, target, sems.at[CHUNKS + i])
        for i, (source, target) in enumerate(((k_hbm, k), (re_hbm, re), (rp_hbm, rp), (q_hbm, q)))
    ]
    chunks = [
        pltpu.make_async_copy(
            table_hbm.at[ROWS * g : ROWS * (g + 1)], table.at[ROWS * g : ROWS * (g + 1)], sems.at[g]
        )
        for g in range(CHUNKS)
    ]
    for copy in copies + chunks:
        copy.start()
    for copy in copies:
        copy.wait()
    fill_weights(q, rp, weights)
    fill_phases(k, re, phase_ref)
    low = lower_half(16)
    for g in range(4):
        if (256 * g) % ROWS == 0:
            chunks[256 * g // ROWS].wait()
        y = jnp.dot(weights[...], table[256 * g : 256 * (g + 1)], preferred_element_type=jnp.float32)
        y = y[:64] + y[64:]
        by_cos, by_sin = y[:32], y[32:]
        real = by_cos[:, :512] - by_sin[:, 512:]
        imag = by_sin[:, :512] + by_cos[:, 512:]
        rows = slice(16 * g, 16 * g + 16)
        for w in range(2):
            for b in range(4):
                re_part = real[16 * w : 16 * w + 16, LANES * b : LANES * (b + 1)]
                im_part = imag[16 * w : 16 * w + 16, LANES * b : LANES * (b + 1)]
                first = jnp.where(low, re_part, pltpu.roll(im_part, HALF, 1))
                second = jnp.where(low, pltpu.roll(re_part, HALF, 1), im_part)
                out_ref[PLACE1[8 * w + 2 * b], rows] = first.astype(out_ref.dtype)
                out_ref[PLACE1[8 * w + 2 * b + 1], rows] = second.astype(out_ref.dtype)


def add_parts(parts_ref, out_ref):
    total = parts_ref[0].astype(jnp.float32)
    for r in range(1, 16):
        total = total + parts_ref[r].astype(jnp.float32)
    packed, header = pack(total)
    for a in range(8):
        out_ref[a, :64] = packed
        out_ref[a, 64:] = header


def bloch(mid_ref, phase_ref, out_ref):
    straight, turned = [], []
    low = lower_half(64)
    for a in range(8):
        x = unpack(mid_ref[PLACE2[a]])
        high = x.astype(jnp.bfloat16).astype(jnp.float32)
        row, turned_row = [], []
        for piece in (high, x - high):
            rolled = pltpu.roll(piece, HALF, 1)
            row.append(piece)
            turned_row.append(jnp.where(low, -rolled, rolled))
        straight.append(jnp.concatenate(row, axis=1).astype(jnp.bfloat16))
        turned.append(jnp.concatenate(turned_row, axis=1).astype(jnp.bfloat16))
    both = jnp.concatenate(straight + turned, axis=0)
    out = jnp.dot(phase_ref[...], both, preferred_element_type=jnp.float32)
    packed, header = pack(out[:, :LANES] + out[:, LANES:])
    for r in range(16):
        out_ref[PLACE3[r], :32] = packed[32 * r : 32 * r + 32]
        out_ref[PLACE3[r], 32:] = header


def place(pieces_ref, out_ref):
    low = lower_half(32)
    for pair in range(8):
        x0 = unpack(pieces_ref[PLACE3[2 * pair]])
        x1 = unpack(pieces_ref[PLACE3[2 * pair + 1]])
        at = LANES * pair
        out_ref[:, at : at + LANES] = jnp.where(low, x0, pltpu.roll(x1, HALF, 1))
        out_ref[:, 1024 + at : 1024 + at + LANES] = jnp.where(low, pltpu.roll(x0, HALF, 1), x1)


def in_vmem(x):
    return pltpu.with_memory_space_constraint(x, pltpu.VMEM)


def per_device(coupling_table, k_points, re_vectors, rp_vectors, q_points):
    vmem = pl.BlockSpec(memory_space=pltpu.VMEM)
    parts, phase = pl.pallas_call(
        wave_sums,
        in_specs=[pl.BlockSpec(memory_space=pl.ANY)] * 5,
        out_specs=[vmem, vmem],
        out_shape=[pltpu.VMEM((16, 64, LANES), jnp.bfloat16), pltpu.VMEM((512, 1024), jnp.bfloat16)],
        scratch_shapes=[
            pltpu.VMEM((1024, 1024), jnp.bfloat16),
            pltpu.VMEM((3, 512), jnp.int32),
            pltpu.VMEM((3, 512), jnp.int32),
            pltpu.VMEM((3, 16), jnp.int32),
            pltpu.SMEM((2, 3), jnp.int32),
            pltpu.VMEM((128, 256), jnp.bfloat16),
            pltpu.SemaphoreType.DMA((CHUNKS + 4,)),
        ],
        name="wave_sums",
    )(coupling_table.reshape(1024, 1024), k_points, re_vectors, rp_vectors, q_points.T)
    parts = lax.all_to_all(parts, "rp", 0, 0, axis_index_groups=[ORDER1], tiled=True)
    mid = pl.pallas_call(
        add_parts,
        in_specs=[vmem],
        out_specs=vmem,
        out_shape=pltpu.VMEM((8, 72, LANES), jnp.int16),
        name="add_parts",
    )(in_vmem(parts))
    mid = lax.all_to_all(mid, "ka", 0, 0, axis_index_groups=[ORDER2], tiled=True)
    pieces = pl.pallas_call(
        bloch,
        in_specs=[vmem, vmem],
        out_specs=vmem,
        out_shape=pltpu.VMEM((16, 40, LANES), jnp.int16),
        name="bloch",
    )(in_vmem(mid), in_vmem(phase))
    pieces = lax.all_to_all(pieces, "rp", 0, 0, axis_index_groups=[ORDER3], tiled=True)
    return pl.pallas_call(
        place,
        in_specs=[vmem],
        out_specs=vmem,
        out_shape=jax.ShapeDtypeStruct((32, 2048), jnp.float32),
        name="place",
    )(in_vmem(pieces))


def solution(mesh):
    placed = (P("ka", "rp", None), P(None, "ka"), P(), P(None, "rp"), P())
    return jax.shard_map(
        per_device, mesh=mesh, in_specs=placed, out_specs=P(("ka", "rp"), None), check_vma=False
    )
```

```python
import math

import jax
import jax.numpy as jnp
from jax import lax
from jax.experimental import pallas as pl
from jax.experimental.pallas import tpu as pltpu
from jax.sharding import PartitionSpec as P

NKG = 16
LANES = 128
HALF = 64
CHUNKS = 1
ROWS = 1024 // CHUNKS
ORDER1 = [13, 12, 15, 14, 11, 10, 9, 8, 5, 2, 7, 6, 3, 4, 1, 0]
ORDER2 = [5, 4, 3, 2, 7, 6, 1, 0]
ORDER3 = [13, 2, 7, 0, 3, 5, 9, 4, 8, 11, 12, 1, 14, 15, 10, 6]
PLACE1 = [ORDER1.index(r) for r in range(16)]
PLACE2 = [ORDER2.index(a) for a in range(8)]
PLACE3 = [ORDER3.index(r) for r in range(16)]
QUARTER = [math.cos(2.0 * math.pi * n / NKG) for n in range(4)] + [0.0]
BITS = 14
SMALLEST = 2.0**-100


def cosine(n):
    m = n & (NKG - 1)
    t = jnp.minimum(m, NKG - m)
    u = jnp.minimum(t, 8 - t)
    value = jnp.full(n.shape, QUARTER[0], jnp.float32)
    for i in range(1, 5):
        value = jnp.where(u == i, jnp.float32(QUARTER[i]), value)
    return jnp.where(t > 4, -value, value)


def lower_half(rows):
    return lax.broadcasted_iota(jnp.int32, (rows, LANES), 1) < HALF


def exact(x):
    return x.astype(jnp.float32).astype(jnp.bfloat16)


def pack(x):
    most = jnp.maximum(jnp.max(jnp.abs(x), axis=0, keepdims=True), SMALLEST)
    exponent = jnp.ceil(jnp.log2(most))
    packed = jnp.round(x * jnp.exp2(BITS - exponent)).astype(jnp.int32).astype(jnp.int16)
    header = jnp.broadcast_to(exponent, (8, LANES)).astype(jnp.int32).astype(jnp.int16)
    return packed, header


def unpack(block):
    rows = block.shape[0] - 8
    exponent = block[rows:].astype(jnp.int32).astype(jnp.float32)
    unit = jnp.exp2(exponent - BITS)[0:1]
    return block[:rows].astype(jnp.int32).astype(jnp.float32) * unit


def fill_weights(q_ref, rp_ref, weights_ref):
    lane = lax.broadcasted_iota(jnp.int32, (16, 256), 1)
    row = lax.broadcasted_iota(jnp.int32, (16, 256), 0)
    spread = jnp.where((lane & 15) == row, 1.0, 0.0).astype(jnp.bfloat16)
    vectors = jnp.dot(exact(rp_ref[...]), spread, preferred_element_type=jnp.float32).astype(jnp.int32)
    own = (lane >> 4) == row
    for q in range(2):
        n = sum(q_ref[q, d] * vectors[d : d + 1] for d in range(3))
        for part, value in enumerate((cosine(n), cosine(n - 4))):
            high = value.astype(jnp.bfloat16).astype(jnp.float32)
            for fine, piece in enumerate((high, value - high)):
                at = 64 * fine + 32 * part + 16 * q
                block = jnp.where(own, jnp.broadcast_to(piece, (16, 256)), 0.0)
                weights_ref[at : at + 16, :] = block.astype(jnp.bfloat16)


def fill_phases(k_ref, re_ref, phase_ref):
    n = lax.dot_general(
        exact(k_ref[...]), exact(re_ref[...]), (((0,), (0,)), ((), ())), preferred_element_type=jnp.float32
    )
    n = n.astype(jnp.int32) & (NKG - 1)
    lane = lax.broadcasted_iota(jnp.int32, (8, LANES), 1)
    tables = [jnp.broadcast_to(cosine(lane - turn)[0:1], (512, LANES)) for turn in (0, 4)]
    for b in range(4):
        index = n[:, LANES * b : LANES * (b + 1)]
        for i, table in enumerate(tables):
            at = 512 * i + LANES * b
            phase_ref[:, at : at + LANES] = jnp.take_along_axis(table, index, axis=1).astype(jnp.bfloat16)


def wave_sums(table_hbm, k_hbm, re_hbm, rp_hbm, q_hbm, out_ref, phase_ref, table, k, re, rp, q, weights, sems):
    copies = [
        pltpu.make_async_copy(source, target, sems.at[CHUNKS + i])
        for i, (source, target) in enumerate(((k_hbm, k), (re_hbm, re), (rp_hbm, rp), (q_hbm, q)))
    ]
    chunks = [
        pltpu.make_async_copy(
            table_hbm.at[ROWS * g : ROWS * (g + 1)], table.at[ROWS * g : ROWS * (g + 1)], sems.at[g]
        )
        for g in range(CHUNKS)
    ]
    for copy in copies + chunks:
        copy.start()
    for copy in copies:
        copy.wait()
    fill_weights(q, rp, weights)
    fill_phases(k, re, phase_ref)
    low = lower_half(16)
    for g in range(4):
        if (256 * g) % ROWS == 0:
            chunks[256 * g // ROWS].wait()
        y = jnp.dot(weights[...], table[256 * g : 256 * (g + 1)], preferred_element_type=jnp.float32)
        y = y[:64] + y[64:]
        by_cos, by_sin = y[:32], y[32:]
        real = by_cos[:, :512] - by_sin[:, 512:]
        imag = by_sin[:, :512] + by_cos[:, 512:]
        rows = slice(16 * g, 16 * g + 16)
        for w in range(2):
            for b in range(4):
                re_part = real[16 * w : 16 * w + 16, LANES * b : LANES * (b + 1)]
                im_part = imag[16 * w : 16 * w + 16, LANES * b : LANES * (b + 1)]
                first = jnp.where(low, re_part, pltpu.roll(im_part, HALF, 1))
                second = jnp.where(low, pltpu.roll(re_part, HALF, 1), im_part)
                out_ref[PLACE1[8 * w + 2 * b], rows] = first.astype(out_ref.dtype)
                out_ref[PLACE1[8 * w + 2 * b + 1], rows] = second.astype(out_ref.dtype)


def add_parts(parts_ref, out_ref):
    total = parts_ref[0].astype(jnp.float32)
    for r in range(1, 16):
        total = total + parts_ref[r].astype(jnp.float32)
    packed, header = pack(total)
    for a in range(8):
        out_ref[a, :64] = packed
        out_ref[a, 64:] = header


def bloch(mid_ref, phase_ref, out_ref):
    straight, turned = [], []
    low = lower_half(64)
    for a in range(8):
        x = unpack(mid_ref[PLACE2[a]])
        high = x.astype(jnp.bfloat16).astype(jnp.float32)
        row, turned_row = [], []
        for piece in (high, x - high):
            rolled = pltpu.roll(piece, HALF, 1)
            row.append(piece)
            turned_row.append(jnp.where(low, -rolled, rolled))
        straight.append(jnp.concatenate(row, axis=1).astype(jnp.bfloat16))
        turned.append(jnp.concatenate(turned_row, axis=1).astype(jnp.bfloat16))
    both = jnp.concatenate(straight + turned, axis=0)
    out = jnp.dot(phase_ref[...], both, preferred_element_type=jnp.float32)
    packed, header = pack(out[:, :LANES] + out[:, LANES:])
    for r in range(16):
        out_ref[PLACE3[r], :32] = packed[32 * r : 32 * r + 32]
        out_ref[PLACE3[r], 32:] = header


def place(pieces_ref, out_ref):
    low = lower_half(32)
    for pair in range(8):
        x0 = unpack(pieces_ref[PLACE3[2 * pair]])
        x1 = unpack(pieces_ref[PLACE3[2 * pair + 1]])
        at = LANES * pair
        out_ref[:, at : at + LANES] = jnp.where(low, x0, pltpu.roll(x1, HALF, 1))
        out_ref[:, 1024 + at : 1024 + at + LANES] = jnp.where(low, pltpu.roll(x0, HALF, 1), x1)


def in_vmem(x):
    return pltpu.with_memory_space_constraint(x, pltpu.VMEM)


def per_device(coupling_table, k_points, re_vectors, rp_vectors, q_points):
    vmem = pl.BlockSpec(memory_space=pltpu.VMEM)
    parts, phase = pl.pallas_call(
        wave_sums,
        in_specs=[pl.BlockSpec(memory_space=pl.ANY)] * 5,
        out_specs=[vmem, vmem],
        out_shape=[pltpu.VMEM((16, 64, LANES), jnp.bfloat16), pltpu.VMEM((512, 1024), jnp.bfloat16)],
        scratch_shapes=[
            pltpu.VMEM((1024, 1024), jnp.bfloat16),
            pltpu.VMEM((3, 512), jnp.int32),
            pltpu.VMEM((3, 512), jnp.int32),
            pltpu.VMEM((3, 16), jnp.int32),
            pltpu.SMEM((2, 3), jnp.int32),
            pltpu.VMEM((128, 256), jnp.bfloat16),
            pltpu.SemaphoreType.DMA((CHUNKS + 4,)),
        ],
        name="wave_sums",
    )(coupling_table.reshape(1024, 1024), k_points, re_vectors, rp_vectors, q_points.T)
    parts = lax.all_to_all(parts, "rp", 0, 0, axis_index_groups=[ORDER1], tiled=True)
    mid = pl.pallas_call(
        add_parts,
        in_specs=[vmem],
        out_specs=vmem,
        out_shape=pltpu.VMEM((8, 72, LANES), jnp.int16),
        name="add_parts",
    )(in_vmem(parts))
    mid = lax.all_to_all(mid, "ka", 0, 0, axis_index_groups=[ORDER2], tiled=True)
    pieces = pl.pallas_call(
        bloch,
        in_specs=[vmem, vmem],
        out_specs=vmem,
        out_shape=pltpu.VMEM((16, 40, LANES), jnp.int16),
        name="bloch",
    )(in_vmem(mid), in_vmem(phase))
    pieces = lax.all_to_all(pieces, "rp", 0, 0, axis_index_groups=[ORDER3], tiled=True)
    return pl.pallas_call(
        place,
        in_specs=[vmem],
        out_specs=vmem,
        out_shape=jax.ShapeDtypeStruct((32, 2048), jnp.float32),
        name="place",
    )(in_vmem(pieces))


def solution(mesh):
    placed = (P("ka", "rp", None), P(None, "ka"), P(), P(None, "rp"), P())
    return jax.shard_map(
        per_device, mesh=mesh, in_specs=placed, out_specs=P(("ka", "rp"), None), check_vma=False
    )
```

```python
import math

import jax
import jax.numpy as jnp
from jax import lax
from jax.experimental import pallas as pl
from jax.experimental.pallas import tpu as pltpu
from jax.sharding import PartitionSpec as P

NKG = 16
LANES = 128
HALF = 64
CHUNKS = 1
ROWS = 1024 // CHUNKS
ORDER1 = [13, 12, 15, 14, 11, 10, 9, 8, 5, 2, 7, 6, 3, 4, 1, 0]
ORDER2 = [5, 4, 3, 7, 2, 6, 1, 0]
ORDER3 = [13, 5, 12, 4, 15, 7, 14, 6, 11, 3, 10, 2, 9, 1, 8, 0]
PLACE1 = [ORDER1.index(r) for r in range(16)]
PLACE2 = [ORDER2.index(a) for a in range(8)]
PLACE3 = [ORDER3.index(r) for r in range(16)]
QUARTER = [math.cos(2.0 * math.pi * n / NKG) for n in range(4)] + [0.0]
BITS = 14
SMALLEST = 2.0**-100


def cosine(n):
    m = n & (NKG - 1)
    t = jnp.minimum(m, NKG - m)
    u = jnp.minimum(t, 8 - t)
    value = jnp.full(n.shape, QUARTER[0], jnp.float32)
    for i in range(1, 5):
        value = jnp.where(u == i, jnp.float32(QUARTER[i]), value)
    return jnp.where(t > 4, -value, value)


def lower_half(rows):
    return lax.broadcasted_iota(jnp.int32, (rows, LANES), 1) < HALF


def exact(x):
    return x.astype(jnp.float32).astype(jnp.bfloat16)


def pack(x):
    most = jnp.maximum(jnp.max(jnp.abs(x), axis=0, keepdims=True), SMALLEST)
    exponent = jnp.ceil(jnp.log2(most))
    packed = jnp.round(x * jnp.exp2(BITS - exponent)).astype(jnp.int32).astype(jnp.int16)
    header = jnp.broadcast_to(exponent, (8, LANES)).astype(jnp.int32).astype(jnp.int16)
    return packed, header


def unpack(block):
    rows = block.shape[0] - 8
    exponent = block[rows:].astype(jnp.int32).astype(jnp.float32)
    unit = jnp.exp2(exponent - BITS)[0:1]
    return block[:rows].astype(jnp.int32).astype(jnp.float32) * unit


def fill_weights(q_ref, rp_ref, weights_ref):
    lane = lax.broadcasted_iota(jnp.int32, (16, 256), 1)
    row = lax.broadcasted_iota(jnp.int32, (16, 256), 0)
    spread = jnp.where((lane & 15) == row, 1.0, 0.0).astype(jnp.bfloat16)
    vectors = jnp.dot(exact(rp_ref[...]), spread, preferred_element_type=jnp.float32).astype(jnp.int32)
    own = (lane >> 4) == row
    for q in range(2):
        n = sum(q_ref[q, d] * vectors[d : d + 1] for d in range(3))
        for part, value in enumerate((cosine(n), cosine(n - 4))):
            high = value.astype(jnp.bfloat16).astype(jnp.float32)
            for fine, piece in enumerate((high, value - high)):
                at = 64 * fine + 32 * part + 16 * q
                block = jnp.where(own, jnp.broadcast_to(piece, (16, 256)), 0.0)
                weights_ref[at : at + 16, :] = block.astype(jnp.bfloat16)


def fill_phases(k_ref, re_ref, phase_ref):
    n = lax.dot_general(
        exact(k_ref[...]), exact(re_ref[...]), (((0,), (0,)), ((), ())), preferred_element_type=jnp.float32
    )
    n = n.astype(jnp.int32) & (NKG - 1)
    lane = lax.broadcasted_iota(jnp.int32, (8, LANES), 1)
    tables = [jnp.broadcast_to(cosine(lane - turn)[0:1], (512, LANES)) for turn in (0, 4)]
    for b in range(4):
        index = n[:, LANES * b : LANES * (b + 1)]
        for i, table in enumerate(tables):
            at = 512 * i + LANES * b
            phase_ref[:, at : at + LANES] = jnp.take_along_axis(table, index, axis=1).astype(jnp.bfloat16)


def wave_sums(table_hbm, k_hbm, re_hbm, rp_hbm, q_hbm, out_ref, phase_ref, table, k, re, rp, q, weights, sems):
    copies = [
        pltpu.make_async_copy(source, target, sems.at[CHUNKS + i])
        for i, (source, target) in enumerate(((k_hbm, k), (re_hbm, re), (rp_hbm, rp), (q_hbm, q)))
    ]
    chunks = [
        pltpu.make_async_copy(
            table_hbm.at[ROWS * g : ROWS * (g + 1)], table.at[ROWS * g : ROWS * (g + 1)], sems.at[g]
        )
        for g in range(CHUNKS)
    ]
    for copy in copies + chunks:
        copy.start()
    for copy in copies:
        copy.wait()
    fill_weights(q, rp, weights)
    fill_phases(k, re, phase_ref)
    low = lower_half(16)
    for g in range(4):
        if (256 * g) % ROWS == 0:
            chunks[256 * g // ROWS].wait()
        y = jnp.dot(weights[...], table[256 * g : 256 * (g + 1)], preferred_element_type=jnp.float32)
        y = y[:64] + y[64:]
        by_cos, by_sin = y[:32], y[32:]
        real = by_cos[:, :512] - by_sin[:, 512:]
        imag = by_sin[:, :512] + by_cos[:, 512:]
        rows = slice(16 * g, 16 * g + 16)
        for w in range(2):
            for b in range(4):
                re_part = real[16 * w : 16 * w + 16, LANES * b : LANES * (b + 1)]
                im_part = imag[16 * w : 16 * w + 16, LANES * b : LANES * (b + 1)]
                first = jnp.where(low, re_part, pltpu.roll(im_part, HALF, 1))
                second = jnp.where(low, pltpu.roll(re_part, HALF, 1), im_part)
                out_ref[PLACE1[8 * w + 2 * b], rows] = first.astype(out_ref.dtype)
                out_ref[PLACE1[8 * w + 2 * b + 1], rows] = second.astype(out_ref.dtype)


def add_parts(parts_ref, out_ref):
    total = parts_ref[0].astype(jnp.float32)
    for r in range(1, 16):
        total = total + parts_ref[r].astype(jnp.float32)
    packed, header = pack(total)
    for a in range(8):
        out_ref[a, :64] = packed
        out_ref[a, 64:] = header


def bloch(mid_ref, phase_ref, out_ref):
    straight, turned = [], []
    low = lower_half(64)
    for a in range(8):
        x = unpack(mid_ref[PLACE2[a]])
        high = x.astype(jnp.bfloat16).astype(jnp.float32)
        row, turned_row = [], []
        for piece in (high, x - high):
            rolled = pltpu.roll(piece, HALF, 1)
            row.append(piece)
            turned_row.append(jnp.where(low, -rolled, rolled))
        straight.append(jnp.concatenate(row, axis=1).astype(jnp.bfloat16))
        turned.append(jnp.concatenate(turned_row, axis=1).astype(jnp.bfloat16))
    both = jnp.concatenate(straight + turned, axis=0)
    out = jnp.dot(phase_ref[...], both, preferred_element_type=jnp.float32)
    packed, header = pack(out[:, :LANES] + out[:, LANES:])
    for r in range(16):
        out_ref[PLACE3[r], :32] = packed[32 * r : 32 * r + 32]
        out_ref[PLACE3[r], 32:] = header


def place(pieces_ref, out_ref):
    low = lower_half(32)
    for pair in range(8):
        x0 = unpack(pieces_ref[PLACE3[2 * pair]])
        x1 = unpack(pieces_ref[PLACE3[2 * pair + 1]])
        at = LANES * pair
        out_ref[:, at : at + LANES] = jnp.where(low, x0, pltpu.roll(x1, HALF, 1))
        out_ref[:, 1024 + at : 1024 + at + LANES] = jnp.where(low, pltpu.roll(x0, HALF, 1), x1)


def in_vmem(x):
    return pltpu.with_memory_space_constraint(x, pltpu.VMEM)


def per_device(coupling_table, k_points, re_vectors, rp_vectors, q_points):
    vmem = pl.BlockSpec(memory_space=pltpu.VMEM)
    parts, phase = pl.pallas_call(
        wave_sums,
        in_specs=[pl.BlockSpec(memory_space=pl.ANY)] * 5,
        out_specs=[vmem, vmem],
        out_shape=[pltpu.VMEM((16, 64, LANES), jnp.bfloat16), pltpu.VMEM((512, 1024), jnp.bfloat16)],
        scratch_shapes=[
            pltpu.VMEM((1024, 1024), jnp.bfloat16),
            pltpu.VMEM((3, 512), jnp.int32),
            pltpu.VMEM((3, 512), jnp.int32),
            pltpu.VMEM((3, 16), jnp.int32),
            pltpu.SMEM((2, 3), jnp.int32),
            pltpu.VMEM((128, 256), jnp.bfloat16),
            pltpu.SemaphoreType.DMA((CHUNKS + 4,)),
        ],
        name="wave_sums",
    )(coupling_table.reshape(1024, 1024), k_points, re_vectors, rp_vectors, q_points.T)
    parts = lax.all_to_all(parts, "rp", 0, 0, axis_index_groups=[ORDER1], tiled=True)
    mid = pl.pallas_call(
        add_parts,
        in_specs=[vmem],
        out_specs=vmem,
        out_shape=pltpu.VMEM((8, 72, LANES), jnp.int16),
        name="add_parts",
    )(in_vmem(parts))
    mid = lax.all_to_all(mid, "ka", 0, 0, axis_index_groups=[ORDER2], tiled=True)
    pieces = pl.pallas_call(
        bloch,
        in_specs=[vmem, vmem],
        out_specs=vmem,
        out_shape=pltpu.VMEM((16, 40, LANES), jnp.int16),
        name="bloch",
    )(in_vmem(mid), in_vmem(phase))
    pieces = lax.all_to_all(pieces, "rp", 0, 0, axis_index_groups=[ORDER3], tiled=True)
    return pl.pallas_call(
        place,
        in_specs=[vmem],
        out_specs=vmem,
        out_shape=jax.ShapeDtypeStruct((32, 2048), jnp.float32),
        name="place",
    )(in_vmem(pieces))


def solution(mesh):
    placed = (P("ka", "rp", None), P(None, "ka"), P(), P(None, "rp"), P())
    return jax.shard_map(
        per_device, mesh=mesh, in_specs=placed, out_specs=P(("ka", "rp"), None), check_vma=False
    )
```
